768 devices in a mesh: space: 192 (over z, y, x_hi), cuts: 4 (over x_lo, core).
Axes of the slice: x: 4 (x_hi: 2, x_lo: 2; x = x_hi * 2 + x_lo), y: 8, z: 12, core: 2. Of those that a mesh axis runs over, the one named last changes fastest.
Arguments:
- vectors: float32 [4, 2, 512, 49152], P('cuts', None, None, 'space'), may hold values from -0.75 to 0.75
- momenta: int32 [3, 3], replicated, may hold values from -3 to 3, as said below
- diagrams: int32 [64, 5], replicated, may hold values from 0 to 3, as said below
Outputs:
- meson: float32 [4, 1536, 1024], P('cuts', 'space')
- diagram_values: float32 [64, 2], replicated
The draws below stay inside these ranges and needn't reach their ends.
Inputs may be any that keep to these rules, and one draw needn't show every extreme that they name: `momenta`: first component of each momentum is nonzero. `diagrams`: column 0 is a tile id below (2)**2, columns 1 and 2 are time slices, column 3 a phase, column 4 the owner index along cuts; no owner is named more than 32 times and one owner exactly 32 times.
All inputs are finite; a program needn't handle non-finite values.
Results may differ from the reference program's by a relative error of at most 0.0003.
Values sent between devices are 32-bit elements; how exact they have to be, the bound alone decides.
A program may use at most 32 MiB of HBM per device.

```python
import math
import jax
import jax.numpy as jnp
from jax import lax

MODES = 512
TILE = 256
PHASES = 3
EXTENT = 96
PRODUCTS = 64
OWN_MOST = 32
SPACE_SITES = 49152
TSLICES = 4


def draw_momenta(key, part):
    keys = jax.random.split(jax.random.fold_in(key, 11), 3)
    position = jnp.arange(PHASES, dtype=jnp.int32)
    magnitude = jax.random.randint(keys[0], (PHASES,), 1, 4)
    magnitude = jnp.where(position < 2, 3, magnitude)
    signs = 2 * jax.random.randint(keys[1], (PHASES,), 0, 2) - 1
    signs = jnp.where(position == 0, 1, jnp.where(position == 1, -1, signs))
    others = jax.random.randint(keys[2], (PHASES, 2), -3, 4)
    return jnp.concatenate([(magnitude * signs)[:, None], others], axis=1).astype(jnp.int32)


def draw_diagrams(key, part):
    keys = jax.random.split(jax.random.fold_in(key, 23), 7)
    tiles = jax.random.randint(keys[0], (PRODUCTS,), 0, MODES // TILE * (MODES // TILE))
    first = jax.random.randint(keys[1], (PRODUCTS,), 0, TSLICES)
    second = jax.random.randint(keys[2], (PRODUCTS,), 0, TSLICES)
    phase = jax.random.randint(keys[3], (PRODUCTS,), 0, PHASES)
    heavy = jax.random.randint(keys[4], (), 0, TSLICES)
    others = (heavy + 1 + jax.random.randint(keys[5], (PRODUCTS,), 0, TSLICES - 1)) % TSLICES
    owner = jnp.where(jnp.arange(PRODUCTS) < OWN_MOST, heavy, others)
    order = jax.random.permutation(keys[6], PRODUCTS)
    owner = owner[order]
    return jnp.stack([tiles, first, second, phase, owner], axis=1).astype(jnp.int32)


def shard_levels(rng, shape, pieces, smallest, top_value):
    gain, own = 1.0, jax.random.fold_in(rng, 6)
    for axis_at, shards_of in pieces:
        draws = jnp.exp(jax.random.uniform(jax.random.fold_in(own, axis_at), (shards_of,), jnp.float32, smallest / len(pieces), top_value / len(pieces)))
        gain = gain * jnp.repeat(draws, shape[axis_at] // shards_of).reshape([-1 if axis == axis_at else 1 for axis in range(len(shape))])
    return gain


def gaussian(stream_key, extent, scale, limit, cuts=(), held_as=jnp.bfloat16):
    gain = shard_levels(stream_key, extent, cuts, -0.22, 0.18) if cuts else 1.0
    array = jax.random.normal(stream_key, extent, jnp.float32) * scale * gain
    return jnp.minimum(jnp.maximum(array, -limit), limit).astype(held_as)


def setup_inputs(seed: int = 0) -> dict:
    arg_keys = jax.random.split(jax.random.key(seed), 4)
    vectors = gaussian(arg_keys[0], (TSLICES, 2, MODES, SPACE_SITES), ((4 * SPACE_SITES) ** -0.25), 0.75, ((0, 4), (3, 192)), jnp.float32)
    momenta = draw_momenta(jax.random.fold_in(arg_keys[3], 71), 0)
    diagrams = draw_diagrams(jax.random.fold_in(arg_keys[3], 71), 0)
    return dict(vectors=vectors, momenta=momenta, diagrams=diagrams)


full_turn = 2.0 * math.pi


def angles_for(moment_rows, site_ids):
    coord_x = site_ids % EXTENT
    coord_y = (site_ids // EXTENT) % EXTENT
    coord_z = site_ids // (EXTENT * EXTENT)
    dotted = moment_rows[:, 0:1] * coord_x[None, :] + moment_rows[:, 1:2] * coord_y[None, :] + moment_rows[:, 2:3] * coord_z[None, :]
    return jnp.mod(dotted, EXTENT).astype(jnp.float32) * (full_turn / EXTENT)


def phased_rows(real_vec, imag_vec, moment_rows, site_ids):
    angle = angles_for(moment_rows, site_ids)
    cosine = jnp.cos(angle)
    sine = jnp.sin(angle)
    left_real = real_vec * cosine + imag_vec * sine
    left_imag = real_vec * sine - imag_vec * cosine
    return jnp.concatenate([left_real, left_imag], axis=1)


def right_block(real_vec, imag_vec):
    upper = jnp.concatenate([real_vec, -imag_vec], axis=1)
    lower = jnp.concatenate([imag_vec, real_vec], axis=1)
    return jnp.concatenate([upper, lower], axis=0)


def contract(left, right):
    return lax.dot_general(left, right, (((1,), (1,)), ((), ())), precision=lax.Precision.HIGHEST, preferred_element_type=jnp.float32)


def tile_columns(rows, column_start):
    real_cols = lax.dynamic_slice_in_dim(rows, column_start, TILE, 1)
    imag_cols = lax.dynamic_slice_in_dim(rows, column_start + MODES, TILE, 1)
    return real_cols, imag_cols


def tile_pair(first_real, first_imag, second_real, second_imag, mask):
    real_rows = jnp.sum(first_real * second_real + first_imag * second_imag, axis=1)
    imag_rows = jnp.sum(first_imag * second_real - first_real * second_imag, axis=1)
    return jnp.stack([jnp.sum(mask * real_rows), jnp.sum(mask * imag_rows)]) / TILE


def reference(vectors, momenta, diagrams):
    site_ids = jnp.arange(SPACE_SITES, dtype=jnp.int32)
    fields = []
    for slice_index in range(TSLICES):
        real_vec = vectors[slice_index, 0]
        imag_vec = vectors[slice_index, 1]
        right = right_block(real_vec, imag_vec)
        blocks = []
        for phase in range(PHASES):
            left = phased_rows(real_vec, imag_vec, momenta[phase:phase + 1], site_ids)
            blocks.append(contract(left, right))
        fields.append(jnp.concatenate(blocks, axis=0))
    meson = jnp.stack(fields)
    tiles_per = MODES // TILE

    def one_product(entry):
        tile_row = entry[0] // tiles_per
        column_start = ((entry[0] % tiles_per) * TILE).astype(jnp.int32)
        row_start = (entry[3] * MODES + tile_row * TILE).astype(jnp.int32)
        first = lax.dynamic_slice_in_dim(lax.dynamic_index_in_dim(meson, entry[1], 0, keepdims=False), row_start, TILE, 0)
        second = lax.dynamic_slice_in_dim(lax.dynamic_index_in_dim(meson, entry[2], 0, keepdims=False), row_start, TILE, 0)
        first_real, first_imag = tile_columns(first, column_start)
        second_real, second_imag = tile_columns(second, column_start)
        return tile_pair(first_real, first_imag, second_real, second_imag, jnp.ones((TILE,), jnp.float32))

    diagram_values = lax.map(one_product, diagrams)
    return meson, diagram_values
```

```python
import functools
import math

import jax
import jax.numpy as jnp
from jax import lax
from jax.experimental import pallas as pl
from jax.experimental.pallas import tpu as pltpu
from jax.sharding import PartitionSpec as P

TILE = 256
PHASES = 3
EXTENT = 96
RINGS = (12, 8, 2)
CUTS = 4
SUBS = 2
HOP_Z, HOP_Y, HOP_SMALL = 2.6, 3.9, 1.6

full_turn = 2.0 * math.pi
MESH = pl.DeviceIdType.MESH


def contract(left, right):
    return lax.dot_general(
        left, right, (((1,), (1,)), ((), ())), preferred_element_type=jnp.float32
    )


def halves(value):
    high = value.astype(jnp.bfloat16)
    low = (value - high.astype(jnp.float32)).astype(jnp.bfloat16)
    return high, low


class Ring:
    def __init__(self, name, extent, hop):
        self.name, self.extent, self.hop = name, extent, hop
        self.hops = (extent // 2, extent - 1 - extent // 2)


def kernel(
    vec_ref,
    mom_ref,
    dia_ref,
    meson_ref,
    value_ref,
    left,
    right,
    a0,
    a1,
    b0,
    b1,
    own_a,
    own_b,
    c0,
    c1,
    d0,
    d1,
    piece,
    got,
    whole,
    total,
    sum_y,
    sum_x,
    sum_z,
    send_a,
    recv_a,
    send_b,
    recv_b,
    send_c,
    recv_c,
    send_d,
    recv_d,
    send_e,
    recv_e,
    send_y,
    recv_y,
    send_x,
    recv_x,
    send_z,
    recv_z,
):
    nz, ny, nx = RINGS
    nc = CUTS
    modes, sites = vec_ref.shape[2:]
    width = modes // SUBS
    rows_y = left.shape[2]
    rows_z = ny * rows_y
    rows_x = rows_y // nx
    quarter = modes // nc
    space = lax.axis_index("space")
    cut = lax.axis_index("cuts")
    x = lax.rem(space, nx)
    y = lax.rem(space // nx, ny)
    z = space // (nx * ny)
    sign = 1 - 2 * lax.rem(cut, 2)

    def at(zz, yy, xx, cc):
        return ((zz * ny + yy) * nx + xx, cc)

    def z_at(step):
        return lax.rem(z + step + 2 * nz, nz)

    def y_at(step):
        return lax.rem(y + step + 2 * ny, ny)

    peers = [at(z_at(k), y, x, cut) for k in range(1, nz)]
    peers += [at(z, y_at(k), x, cut) for k in range(1, ny)]
    others = [
        (lax.rem(x + dx, nx), lax.rem(cut + dc, nc), dx, dc)
        for dx in range(nx)
        for dc in range(nc)
        if dx or dc
    ]
    peers += [at(z, y, xx, cc) for xx, cc, _, _ in others]
    barrier = pltpu.get_barrier_semaphore()
    for peer in peers:
        pl.semaphore_signal(barrier, inc=1, device_id=peer, device_id_type=MESH)

    real_vec = vec_ref[0, 0]
    imag_vec = vec_ref[0, 1]
    depth = 2 * sites
    rh, rl = halves(real_vec)
    ih, il = halves(imag_vec)
    for part, (first, second) in enumerate((((rh, rl), (-ih, -il)), ((ih, il), (rh, rl)))):
        rows = slice(part * modes, (part + 1) * modes)
        for place, (high, low) in enumerate((first, second)):
            cols = place * sites
            right[rows, cols : cols + sites] = high
            right[rows, depth + cols : depth + cols + sites] = high
            right[rows, 2 * depth + cols : 2 * depth + cols + sites] = low

    lane = lax.broadcasted_iota(jnp.int32, (1, sites), 1)
    site = (space * sites + lane).astype(jnp.float32)
    line = jnp.floor((site + 0.5) * (1.0 / EXTENT))
    coord_x = site - line * EXTENT
    coord_z = jnp.floor((line + 0.5) * (1.0 / EXTENT))
    coord_y = line - coord_z * EXTENT
    blocks = modes // rows_y
    for phase in range(PHASES):
        dotted = (
            mom_ref[phase, 0].astype(jnp.float32) * coord_x
            + mom_ref[phase, 1].astype(jnp.float32) * coord_y
            + mom_ref[phase, 2].astype(jnp.float32) * coord_z
        )
        turned = dotted - jnp.floor((dotted + 0.5) * (1.0 / EXTENT)) * EXTENT
        angle = turned * (full_turn / EXTENT)
        cosine = jnp.cos(angle)
        sine = jnp.sin(angle)
        for place, value in enumerate(
            (real_vec * cosine + imag_vec * sine, real_vec * sine - imag_vec * cosine)
        ):
            high, low = halves(value)
            cols = place * sites
            for block in range(blocks):
                zz, yy = divmod(phase * blocks + block, ny)
                rows = slice(block * rows_y, (block + 1) * rows_y)
                left[zz, yy, :, cols : cols + sites] = high[rows]
                left[zz, yy, :, depth + cols : depth + cols + sites] = low[rows]
                left[zz, yy, :, 2 * depth + cols : 2 * depth + cols + sites] = high[rows]

    pl.semaphore_wait(barrier, len(peers))
    sends = []

    def post(source, target, send_sem, recv_sem, peer):
        copy = pltpu.make_async_remote_copy(
            src_ref=source,
            dst_ref=target,
            send_sem=send_sem,
            recv_sem=recv_sem,
            device_id=peer,
            device_id_type=MESH,
        )
        copy.start()
        sends.append(copy)

    def arrived(target, send_sem, recv_sem):
        pltpu.make_async_remote_copy(
            src_ref=target,
            dst_ref=target,
            send_sem=send_sem,
            recv_sem=recv_sem,
            device_id=at(z, y, x, cut),
            device_id_type=MESH,
        ).wait_recv()

    def local_a(zz, sub):
        rows = left[zz].reshape(rows_z, left.shape[3])
        return contract(rows, right[sub * width : (sub + 1) * width, :])

    def local_b(yy, sub):
        rows = left[:, yy].reshape(nz * rows_y, left.shape[3])
        start = modes + sub * width
        return contract(rows, right[start : start + width, :])

    def ring(ring_of, slots, send_sems, recv_sems, sub, local, finish, step_at, peer_of, start, tick):
        hops = ring_of.hops

        def hop(direction, step):
            way = sign if direction == 0 else -sign
            buffer = slots[direction]
            here = buffer.at[step, sub]
            if step:
                mine = local(step_at(way * (hops[direction] - step)), sub)
                arrived(here, send_sems.at[direction, step - 1, sub], recv_sems.at[direction, step - 1, sub])
                here[...] += mine
            else:
                here[...] = local(step_at(way * hops[direction]), sub)
            post(
                here,
                buffer.at[step + 1, sub],
                send_sems.at[direction, step, sub],
                recv_sems.at[direction, step, sub],
                peer_of(way),
            )

        def last():
            value = local(step_at(0), sub)
            for direction in (0, 1):
                count = hops[direction]
                if count:
                    here = slots[direction].at[count, sub]
                    arrived(here, send_sems.at[direction, count - 1, sub], recv_sems.at[direction, count - 1, sub])
                    value += here[...]
            finish(sub, value)

        for direction in (0, 1):
            for step in range(hops[direction]):
                yield start + tick * (step * SUBS + sub), functools.partial(hop, direction, step)
        yield start + tick * (hops[0] * SUBS + sub), last

    def z_peer(way):
        return at(z_at(way), y, x, cut)

    def y_peer(way):
        return at(z, y_at(way), x, cut)

    ring_z = Ring("z", nz, HOP_Z)
    ring_y = Ring("y", ny, HOP_Y)

    def keep_a(sub, value):
        own_a[sub] = value.reshape(ny, rows_y, width)

    def keep_b(sub, value):
        own_b[sub] = value.reshape(nz, rows_y, width)

    per = width // quarter

    def keep_piece(part):
        def keep(sub, value):
            for xx in range(nx):
                for k in range(per):
                    piece[xx, sub * per + k, part] = value[
                        xx * rows_x : (xx + 1) * rows_x, k * quarter : (k + 1) * quarter
                    ]

        return keep

    end_a = HOP_Z * SUBS * ring_z.hops[0]
    end_b = HOP_Y * SUBS * ring_y.hops[0]
    events = []
    for sub in range(SUBS):
        events += ring(
            ring_z, (a0, a1), send_a, recv_a, sub, local_a, keep_a, z_at, z_peer, 0.0, HOP_Z
        )
        events += ring(
            ring_y, (b0, b1), send_b, recv_b, sub, local_b, keep_b, y_at, y_peer, 0.01, HOP_Y
        )
        events += ring(
            ring_y, (c0, c1), send_c, recv_c, sub, lambda yy, s: own_a[s, yy], keep_piece(0),
            y_at, y_peer, end_a + HOP_Z * sub + 0.1, HOP_SMALL / SUBS,
        )
        events += ring(
            ring_z, (d0, d1), send_d, recv_d, sub, lambda zz, s: own_b[s, zz], keep_piece(1),
            z_at, z_peer, end_b + HOP_Y * sub + 0.1, HOP_SMALL / SUBS,
        )
    for _, event in sorted(events, key=lambda pair: pair[0]):
        event()

    for xx, cc, dx, dc in others:
        if dc == 0:
            post(piece.at[xx], whole, send_e.at[dx, dc], recv_e.at[dx, dc], at(z, y, xx, cc))
        else:
            post(piece.at[xx, cc], got.at[dx, dc], send_e.at[dx, dc], recv_e.at[dx, dc], at(z, y, xx, cc))

    entries = dia_ref.shape[0]
    lanes = sum_y.shape[2]
    tile_id = dia_ref[:, 0:1]
    tile_row = tile_id >> 1
    tile_col = tile_id & 1
    key_lane = (dia_ref[:, 3:4] * 2 + tile_row) * (nc * nc) + dia_ref[:, 1:2] * nc + dia_ref[:, 2:3]
    is_lane = lax.broadcasted_iota(jnp.int32, (entries, lanes), 1) == key_lane
    pick = [is_lane & (tile_col == b) for b in range(2)]

    for dc in range(nc):
        if dc:
            for dx in range(nx):
                arrived(got.at[dx, dc], send_e.at[dx, dc], recv_e.at[dx, dc])
            value = got[0, dc]
            for dx in range(1, nx):
                value += got[dx, dc]
            total[lax.rem(cut - dc + nc, nc)] = value
        elif nx > 1:
            arrived(whole, send_e.at[1, 0], recv_e.at[1, 0])
            whole[...] += piece[x]
        else:
            whole[...] = piece[x]
    total[cut] = whole[cut]

    re = [total[t, 0] for t in range(nc)]
    im = [total[t, 1] for t in range(nc)]

    def down(value):
        return jnp.sum(value, axis=0, keepdims=True)

    rr, ii = {}, {}
    for s in range(nc):
        for t in range(s, nc):
            rr[s, t] = rr[t, s] = down(re[s] * re[t] + im[s] * im[t])
            if s == t:
                ii[s, t] = jnp.zeros_like(rr[s, t])
            else:
                ii[s, t] = down(im[s] * re[t] - re[s] * im[t])
                ii[t, s] = -ii[s, t]
    pairs = [(s, t) for s in range(nc) for t in range(nc)]
    key = z // (nz // (2 * PHASES))
    own_b_col = cut // 2
    lane_id = lax.broadcasted_iota(jnp.int32, (nc * nc, lanes), 1)
    row_id = lax.broadcasted_iota(jnp.int32, (nc * nc, lanes), 0)
    spot = lane_id == key * (nc * nc) + row_id
    tile_rows = lax.broadcasted_iota(jnp.int32, sum_y.shape[1:], 0)
    table = jnp.zeros(sum_y.shape[1:], jnp.float32)
    for part, values in enumerate((rr, ii)):
        column = jnp.sum(jnp.concatenate([values[p] for p in pairs], axis=0), axis=1, keepdims=True)
        lane_row = down(jnp.where(spot, column, 0.0))
        table = jnp.where(tile_rows == 2 * part + own_b_col, lane_row, table)

    def all_sum(table, slots, send_sems, recv_sems, me, count, targets):
        slots[me] = table
        for k, peer in enumerate(targets):
            post(slots.at[me], slots.at[me], send_sems.at[k], recv_sems.at[me], peer)
        for k in range(1, count):
            source = lax.rem(me + k, count)
            arrived(slots.at[source], send_sems.at[k - 1], recv_sems.at[source])
        value = slots[0]
        for k in range(1, count):
            value += slots[k]
        return value

    table = all_sum(table, sum_y, send_y, recv_y, y, ny, [at(z, y_at(k), x, cut) for k in range(1, ny)])

    for part in range(2):
        for k in range(nc):
            start = part * modes + k * quarter
            meson_ref[0, :, start : start + quarter] = whole[k, part]

    table = all_sum(
        table, sum_x, send_x, recv_x, x * nc + cut, nx * nc, [at(z, y, xx, cc) for xx, cc, _, _ in others]
    )
    table = all_sum(table, sum_z, send_z, recv_z, z, nz, [at(z_at(k), y, x, cut) for k in range(1, nz)])

    columns = []
    for part in range(2):
        value = jnp.where(pick[0], table[2 * part : 2 * part + 1], 0.0) + jnp.where(
            pick[1], table[2 * part + 1 : 2 * part + 2], 0.0
        )
        columns.append(jnp.sum(value, axis=1, keepdims=True) / TILE)
    value_ref[...] = jnp.concatenate(columns, axis=1)

    for copy in sends:
        copy.wait_send()


def per_device(vectors, momenta, diagrams):
    nz, ny, nx = RINGS
    modes, sites = vectors.shape[2:]
    rows = PHASES * modes
    rows_y = rows // (nz * ny)
    rows_z = rows_y * ny
    width = modes // SUBS
    quarter = modes // CUTS
    lanes = max(128, 2 * PHASES * CUTS * CUTS)
    depth = 6 * sites
    z_hops = Ring("z", nz, HOP_Z).hops
    y_hops = Ring("y", ny, HOP_Y).hops
    f32, bf16 = jnp.float32, jnp.bfloat16
    dma = pltpu.SemaphoreType.DMA

    def slots(hops, *shape):
        return [pltpu.VMEM((count + 1, SUBS, *shape), f32) for count in hops]

    def sems(hops):
        return [dma((2, hops[0], SUBS))] * 2

    scratch = [
        pltpu.VMEM((nz, ny, rows_y, depth), bf16),
        pltpu.VMEM((2 * modes, depth), bf16),
        *slots(z_hops, rows_z, width),
        *slots(y_hops, nz * rows_y, width),
        pltpu.VMEM((SUBS, ny, rows_y, width), f32),
        pltpu.VMEM((SUBS, nz, rows_y, width), f32),
        *slots(y_hops, rows_y, width),
        *slots(z_hops, rows_y, width),
        pltpu.VMEM((nx, CUTS, 2, rows_y // nx, quarter), f32),
        pltpu.VMEM((nx, CUTS, 2, rows_y // nx, quarter), f32),
        pltpu.VMEM((CUTS, 2, rows_y // nx, quarter), f32),
        pltpu.VMEM((CUTS, 2, rows_y // nx, quarter), f32),
        pltpu.VMEM((ny, 8, lanes), f32),
        pltpu.VMEM((nx * CUTS, 8, lanes), f32),
        pltpu.VMEM((nz, 8, lanes), f32),
        *sems(z_hops),
        *sems(y_hops),
        *sems(y_hops),
        *sems(z_hops),
        *[dma((nx, CUTS))] * 2,
        *[dma((ny,))] * 2,
        *[dma((nx * CUTS,))] * 2,
        *[dma((nz,))] * 2,
    ]
    vmem = pl.BlockSpec(memory_space=pltpu.VMEM)
    return pl.pallas_call(
        kernel,
        out_shape=(
            jax.ShapeDtypeStruct((1, rows_y // nx, 2 * modes), f32),
            jax.ShapeDtypeStruct((diagrams.shape[0], 2), f32),
        ),
        in_specs=[vmem, pl.BlockSpec(memory_space=pltpu.SMEM), vmem],
        out_specs=(vmem, vmem),
        scratch_shapes=scratch,
        compiler_params=pltpu.CompilerParams(
            collective_id=0, has_side_effects=True, vmem_limit_bytes=56 * 1024 * 1024
        ),
    )(vectors, momenta, diagrams)


def solution(mesh):
    return jax.shard_map(
        per_device,
        mesh=mesh,
        in_specs=(P("cuts", None, None, "space"), P(), P()),
        out_specs=(P("cuts", "space", None), P()),
        check_vma=False,
    )
```

```python
import functools
import math

import jax
import jax.numpy as jnp
from jax import lax
from jax.experimental import pallas as pl
from jax.experimental.pallas import tpu as pltpu
from jax.sharding import PartitionSpec as P

TILE = 256
PHASES = 3
EXTENT = 96
RINGS = (12, 8, 2)
CUTS = 4
SUBS = 2
HOP_Z, HOP_Y, ROUND = 2.6, 3.9, 4.0
RELAY = 3

full_turn = 2.0 * math.pi
MESH = pl.DeviceIdType.MESH


def contract(left, right):
    return lax.dot_general(
        left, right, (((1,), (1,)), ((), ())), preferred_element_type=jnp.float32
    )


def halves(value):
    high = value.astype(jnp.bfloat16)
    low = (value - high.astype(jnp.float32)).astype(jnp.bfloat16)
    return high, low


def meet(extent):
    return extent // 2, extent - 1 - extent // 2


def far_first(extent):
    return sorted(range(1, extent), key=lambda k: -min(k, extent - k))


def relays(extent):
    by_relay, straight = [], []
    for side, count in enumerate(meet(extent)):
        for distance in range(1, count + 1):
            (by_relay if distance > RELAY else straight).append((side, distance))
    return by_relay, straight


def kernel(
    vec_hbm,
    mom_ref,
    dia_ref,
    meson_ref,
    value_ref,
    vec_ref,
    left,
    right,
    a0,
    a1,
    b0,
    b1,
    own_a,
    own_b,
    in_c,
    relay_d,
    in_d,
    piece,
    got,
    whole,
    total,
    sum_y,
    sum_x,
    sum_z,
    load_sem,
    send_a,
    recv_a,
    send_b,
    recv_b,
    send_c,
    recv_c,
    send_d,
    recv_relay,
    recv_d,
    send_e,
    recv_e,
    send_whole,
    recv_whole,
    send_y,
    recv_y,
    send_x,
    recv_x,
    send_z,
    recv_z,
):
    nz, ny, nx = RINGS
    nc = CUTS
    modes, sites = vec_ref.shape[1:]
    width = modes // SUBS
    rows_y = left.shape[2]
    rows_z = ny * rows_y
    rows_x = rows_y // nx
    quarter = modes // nc
    space = lax.axis_index("space")
    cut = lax.axis_index("cuts")
    x = lax.rem(space, nx)
    y = lax.rem(space // nx, ny)
    z = space // (nx * ny)
    sign = 1 - 2 * lax.rem(cut, 2)

    def at(zz, yy, xx, cc):
        return ((zz * ny + yy) * nx + xx, cc)

    def z_at(step):
        return lax.rem(z + step + 2 * nz, nz)

    def y_at(step):
        return lax.rem(y + step + 2 * ny, ny)

    load = pltpu.make_async_copy(vec_hbm.at[0], vec_ref, load_sem)
    load.start()

    peers = [at(z_at(k), y, x, cut) for k in range(1, nz)]
    peers += [at(z, y_at(k), x, cut) for k in range(1, ny)]
    others = [
        (lax.rem(x + dx, nx), lax.rem(cut + dc, nc), dx, dc)
        for dx in reversed(range(nx))
        for dc in (2, 1, 3, 0)
        if dx or dc
    ]
    peers += [at(z, y, xx, cc) for xx, cc, _, _ in others]
    barrier = pltpu.get_barrier_semaphore()
    for peer in peers:
        pl.semaphore_signal(barrier, inc=1, device_id=peer, device_id_type=MESH)

    load.wait()
    real_vec = vec_ref[0]
    imag_vec = vec_ref[1]
    depth = 2 * sites
    rh, rl = halves(real_vec)
    ih, il = halves(imag_vec)
    for part, (first, second) in enumerate((((rh, rl), (-ih, -il)), ((ih, il), (rh, rl)))):
        rows = slice(part * modes, (part + 1) * modes)
        for place, (high, low) in enumerate((first, second)):
            cols = place * sites
            right[rows, cols : cols + sites] = high
            right[rows, depth + cols : depth + cols + sites] = high
            right[rows, 2 * depth + cols : 2 * depth + cols + sites] = low

    lane = lax.broadcasted_iota(jnp.int32, (1, sites), 1)
    site = (space * sites + lane).astype(jnp.float32)
    line = jnp.floor((site + 0.5) * (1.0 / EXTENT))
    coord_x = site - line * EXTENT
    coord_z = jnp.floor((line + 0.5) * (1.0 / EXTENT))
    coord_y = line - coord_z * EXTENT
    blocks = modes // rows_y
    for phase in range(PHASES):
        dotted = (
            mom_ref[phase, 0].astype(jnp.float32) * coord_x
            + mom_ref[phase, 1].astype(jnp.float32) * coord_y
            + mom_ref[phase, 2].astype(jnp.float32) * coord_z
        )
        turned = dotted - jnp.floor((dotted + 0.5) * (1.0 / EXTENT)) * EXTENT
        angle = turned * (full_turn / EXTENT)
        cosine = jnp.cos(angle)
        sine = jnp.sin(angle)
        for place, value in enumerate(
            (real_vec * cosine + imag_vec * sine, real_vec * sine - imag_vec * cosine)
        ):
            high, low = halves(value)
            cols = place * sites
            for block in range(blocks):
                zz, yy = divmod(phase * blocks + block, ny)
                rows = slice(block * rows_y, (block + 1) * rows_y)
                left[zz, yy, :, cols : cols + sites] = high[rows]
                left[zz, yy, :, depth + cols : depth + cols + sites] = low[rows]
                left[zz, yy, :, 2 * depth + cols : 2 * depth + cols + sites] = high[rows]

    sends = []

    def post(source, target, send_sem, recv_sem, peer):
        copy = pltpu.make_async_remote_copy(
            src_ref=source,
            dst_ref=target,
            send_sem=send_sem,
            recv_sem=recv_sem,
            device_id=peer,
            device_id_type=MESH,
        )
        copy.start()
        sends.append(copy)

    def arrived(target, send_sem, recv_sem):
        pltpu.make_async_remote_copy(
            src_ref=target,
            dst_ref=target,
            send_sem=send_sem,
            recv_sem=recv_sem,
            device_id=at(z, y, x, cut),
            device_id_type=MESH,
        ).wait_recv()

    def local_a(zz, sub):
        rows = left[zz].reshape(rows_z, left.shape[3])
        return contract(rows, right[sub * width : (sub + 1) * width, :])

    def local_b(yy, sub):
        rows = left[:, yy].reshape(nz * rows_y, left.shape[3])
        start = modes + sub * width
        return contract(rows, right[start : start + width, :])

    def ring(hops, slots, send_sems, recv_sems, sub, local, finish, step_at, peer_of, tick):
        def hop(direction, step):
            way = sign if direction == 0 else -sign
            here = slots[direction].at[step, sub]
            if step:
                mine = local(step_at(way * (hops[direction] - step)), sub)
                arrived(here, send_sems.at[direction, step - 1, sub], recv_sems.at[direction, step - 1, sub])
                here[...] += mine
            post(
                here,
                slots[direction].at[step + 1, sub],
                send_sems.at[direction, step, sub],
                recv_sems.at[direction, step, sub],
                peer_of(way),
            )

        def last():
            value = local(step_at(0), sub)
            for direction in (0, 1):
                count = hops[direction]
                if count:
                    here = slots[direction].at[count, sub]
                    arrived(here, send_sems.at[direction, count - 1, sub], recv_sems.at[direction, count - 1, sub])
                    value += here[...]
            finish(sub, value)

        made = []
        for direction in (0, 1):
            for step in range(hops[direction]):
                made.append((tick * (step * SUBS + sub), functools.partial(hop, direction, step)))
        made.append((tick * (hops[0] * SUBS + sub), last))
        return made

    def first_chunks(hops, slots, sub, local, step_at):
        for direction in (0, 1):
            if hops[direction]:
                way = sign if direction == 0 else -sign
                slots[direction][0, sub] = local(step_at(way * hops[direction]), sub)

    def z_peer(way):
        return at(z_at(way), y, x, cut)

    def y_peer(way):
        return at(z, y_at(way), x, cut)

    def way_of(side):
        return sign if side == 0 else -sign

    hops_z, hops_y = meet(nz), meet(ny)
    per = width // quarter

    def keep(part, sub, value):
        for xx in range(nx):
            for k in range(per):
                piece[xx, sub * per + k, part] = value[
                    xx * rows_x : (xx + 1) * rows_x, k * quarter : (k + 1) * quarter
                ]

    def spread_a(sub, value):
        own_a[sub] = value.reshape(ny, rows_y, width)
        for k in far_first(ny):
            post(
                own_a.at[sub, y_at(k)], in_c.at[sub, k - 1], send_c.at[sub, k - 1], recv_c.at[sub, k - 1], y_peer(k)
            )

    def gather_a(sub):
        value = own_a[sub, y]
        for k in far_first(ny)[::-1]:
            arrived(in_c.at[sub, k - 1], send_c.at[sub, k - 1], recv_c.at[sub, k - 1])
            value += in_c[sub, k - 1]
        keep(0, sub, value)

    by_relay, straight = relays(nz)

    def spread_b(sub, value):
        own_b[sub] = value.reshape(nz, rows_y, width)
        for k, (side, distance) in sorted(enumerate(by_relay), key=lambda item: -item[1][1]):
            way = way_of(side)
            post(
                own_b.at[sub, z_at(-way * distance)],
                relay_d.at[sub, k],
                send_d.at[sub, k],
                recv_relay.at[sub, k],
                z_peer(-way * (distance - RELAY)),
            )
        for k, (side, distance) in sorted(enumerate(straight), key=lambda item: -item[1][1]):
            if not has_relay(side, distance):
                send_straight(sub, k, side, distance)

    def has_relay(side, distance):
        return distance == RELAY and any(other == side for other, _ in by_relay)

    def send_straight(sub, k, side, distance):
        way = way_of(side)
        post(
            own_b.at[sub, z_at(-way * distance)],
            in_d.at[sub, k],
            send_d.at[sub, len(by_relay) + k],
            recv_d.at[sub, k],
            z_peer(-way * distance),
        )

    def relay_b(sub):
        for k, (side, distance) in enumerate(straight):
            if has_relay(side, distance):
                spot = z_at(-way_of(side) * distance)
                value = own_b[sub, spot]
                for j, (other, _) in enumerate(by_relay):
                    if other == side:
                        arrived(relay_d.at[sub, j], send_d.at[sub, j], recv_relay.at[sub, j])
                        value += relay_d[sub, j]
                own_b[sub, spot] = value
                send_straight(sub, k, side, distance)

    def gather_b(sub):
        value = own_b[sub, z]
        for k, (side, distance) in enumerate(straight):
            arrived(in_d.at[sub, k], send_d.at[sub, len(by_relay) + k], recv_d.at[sub, k])
            value += in_d[sub, k]
        keep(1, sub, value)

    events = []
    for sub in range(SUBS):
        first_chunks(hops_z, (a0, a1), sub, local_a, z_at)
        first_chunks(hops_y, (b0, b1), sub, local_b, y_at)
        events += ring(hops_z, (a0, a1), send_a, recv_a, sub, local_a, spread_a, z_at, z_peer, HOP_Z)
        end = events[-1][0]
        events.append((end + 1.5 * ROUND, functools.partial(gather_a, sub)))
        events += ring(hops_y, (b0, b1), send_b, recv_b, sub, local_b, spread_b, y_at, y_peer, HOP_Y)
        end = events[-1][0]
        events.append((end + ROUND, functools.partial(relay_b, sub)))
        events.append((end + 2 * ROUND, functools.partial(gather_b, sub)))

    pl.semaphore_wait(barrier, len(peers))
    for _, event in sorted(events, key=lambda pair: pair[0]):
        event()

    for xx, cc, dx, dc in others:
        post(piece.at[xx, cc], got.at[dx, dc], send_e.at[dx, dc], recv_e.at[dx, dc], at(z, y, xx, cc))
    for dx in range(1, nx):
        xx = lax.rem(x + dx, nx)
        post(piece.at[xx], whole.at[dx], send_whole.at[dx], recv_whole.at[dx], at(z, y, xx, cut))

    entries = dia_ref.shape[1]
    lanes = sum_y.shape[2]
    tile_id = dia_ref[0:1, :]
    code = (
        (dia_ref[3:4, :] * 2 + (tile_id >> 1)) * (nc * nc)
        + dia_ref[1:2, :] * nc
        + dia_ref[2:3, :]
        + (tile_id & 1) * lanes
    ).astype(jnp.float32)
    eye = lax.broadcasted_iota(jnp.int32, (entries, entries), 0) == lax.broadcasted_iota(
        jnp.int32, (entries, entries), 1
    )
    code = jnp.sum(jnp.where(eye, code, 0.0), axis=1, keepdims=True)
    lane_code = lax.broadcasted_iota(jnp.int32, (entries, lanes), 1).astype(jnp.float32)
    pick = [lane_code + float(b * lanes) == code for b in range(2)]

    for dc in range(nc):
        for dx in range(nx):
            if dx or dc:
                arrived(got.at[dx, dc], send_e.at[dx, dc], recv_e.at[dx, dc])
        value = got[0, dc] if dc else piece[x, cut]
        for dx in range(1, nx):
            value += got[dx, dc]
        total[lax.rem(cut - dc + nc, nc)] = value

    re = [total[t, 0] for t in range(nc)]
    im = [total[t, 1] for t in range(nc)]

    def down(value):
        return jnp.sum(value, axis=0, keepdims=True)

    rr, ii = {}, {}
    for s in range(nc):
        for t in range(s, nc):
            rr[s, t] = rr[t, s] = down(re[s] * re[t] + im[s] * im[t])
            if s == t:
                ii[s, t] = jnp.zeros_like(rr[s, t])
            else:
                ii[s, t] = down(im[s] * re[t] - re[s] * im[t])
                ii[t, s] = -ii[s, t]
    pairs = [(s, t) for s in range(nc) for t in range(nc)]
    key = z // (nz // (2 * PHASES))
    own_b_col = cut // 2
    lane_id = lax.broadcasted_iota(jnp.int32, (nc * nc, lanes), 1)
    row_id = lax.broadcasted_iota(jnp.int32, (nc * nc, lanes), 0)
    spot = lane_id == key * (nc * nc) + row_id
    tile_rows = lax.broadcasted_iota(jnp.int32, sum_y.shape[1:], 0)
    table = jnp.zeros(sum_y.shape[1:], jnp.float32)
    for part, values in enumerate((rr, ii)):
        column = jnp.sum(jnp.concatenate([values[p] for p in pairs], axis=0), axis=1, keepdims=True)
        lane_row = down(jnp.where(spot, column, 0.0))
        table = jnp.where(tile_rows == 2 * part + own_b_col, lane_row, table)

    def all_sum(table, slots, send_sems, recv_sems, me, count, targets):
        slots[me] = table
        for k, peer in enumerate(targets):
            post(slots.at[me], slots.at[me], send_sems.at[k], recv_sems.at[me], peer)
        for k in range(1, count):
            source = lax.rem(me + k, count)
            arrived(slots.at[source], send_sems.at[k - 1], recv_sems.at[source])
        value = slots[0]
        for k in range(1, count):
            value += slots[k]
        return value

    table = all_sum(table, sum_y, send_y, recv_y, y, ny, [at(z, y_at(k), x, cut) for k in far_first(ny)])

    rows_own = piece[x]
    for dx in range(1, nx):
        arrived(whole.at[dx], send_whole.at[dx], recv_whole.at[dx])
        rows_own += whole[dx]
    for part in range(2):
        for k in range(nc):
            start = part * modes + k * quarter
            meson_ref[0, :, start : start + quarter] = rows_own[k, part]

    table = all_sum(
        table, sum_x, send_x, recv_x, x * nc + cut, nx * nc, [at(z, y, xx, cc) for xx, cc, _, _ in others]
    )
    table = all_sum(table, sum_z, send_z, recv_z, z, nz, [at(z_at(k), y, x, cut) for k in far_first(nz)])

    for part in range(2):
        value = jnp.where(pick[0], table[2 * part : 2 * part + 1], 0.0) + jnp.where(
            pick[1], table[2 * part + 1 : 2 * part + 2], 0.0
        )
        column = jnp.sum(value, axis=1, keepdims=True)
        value_ref[part : part + 1, :] = down(jnp.where(eye, column, 0.0)) / TILE

    for copy in sends:
        copy.wait_send()


def per_device(vectors, momenta, diagrams):
    nz, ny, nx = RINGS
    modes, sites = vectors.shape[2:]
    rows = PHASES * modes
    rows_y = rows // (nz * ny)
    rows_z = rows_y * ny
    width = modes // SUBS
    quarter = modes // CUTS
    lanes = max(128, 2 * PHASES * CUTS * CUTS)
    depth = 6 * sites
    z_hops, y_hops = meet(nz), meet(ny)
    by_relay, straight = relays(nz)
    f32, bf16 = jnp.float32, jnp.bfloat16
    dma = pltpu.SemaphoreType.DMA

    def slots(hops, *shape):
        return [pltpu.VMEM((count + 1, SUBS, *shape), f32) for count in hops]

    def sems(hops):
        return [dma((2, hops[0], SUBS))] * 2

    scratch = [
        pltpu.VMEM(vectors.shape[1:], f32),
        pltpu.VMEM((nz, ny, rows_y, depth), bf16),
        pltpu.VMEM((2 * modes, depth), bf16),
        *slots(z_hops, rows_z, width),
        *slots(y_hops, nz * rows_y, width),
        pltpu.VMEM((SUBS, ny, rows_y, width), f32),
        pltpu.VMEM((SUBS, nz, rows_y, width), f32),
        pltpu.VMEM((SUBS, ny - 1, rows_y, width), f32),
        pltpu.VMEM((SUBS, max(1, len(by_relay)), rows_y, width), f32),
        pltpu.VMEM((SUBS, len(straight), rows_y, width), f32),
        pltpu.VMEM((nx, CUTS, 2, rows_y // nx, quarter), f32),
        pltpu.VMEM((nx, CUTS, 2, rows_y // nx, quarter), f32),
        pltpu.VMEM((nx, CUTS, 2, rows_y // nx, quarter), f32),
        pltpu.VMEM((CUTS, 2, rows_y // nx, quarter), f32),
        pltpu.VMEM((ny, 8, lanes), f32),
        pltpu.VMEM((nx * CUTS, 8, lanes), f32),
        pltpu.VMEM((nz, 8, lanes), f32),
        dma,
        *sems(z_hops),
        *sems(y_hops),
        *[dma((SUBS, ny - 1))] * 2,
        dma((SUBS, nz - 1)),
        dma((SUBS, max(1, len(by_relay)))),
        dma((SUBS, len(straight))),
        *[dma((nx, CUTS))] * 2,
        *[dma((nx,))] * 2,
        *[dma((ny,))] * 2,
        *[dma((nx * CUTS,))] * 2,
        *[dma((nz,))] * 2,
    ]
    vmem = pl.BlockSpec(memory_space=pltpu.VMEM)
    meson, values = pl.pallas_call(
        kernel,
        out_shape=(
            jax.ShapeDtypeStruct((1, rows_y // nx, 2 * modes), f32),
            jax.ShapeDtypeStruct((2, diagrams.shape[0]), f32),
        ),
        in_specs=[pl.BlockSpec(memory_space=pl.ANY), pl.BlockSpec(memory_space=pltpu.SMEM), vmem],
        out_specs=(vmem, vmem),
        scratch_shapes=scratch,
        compiler_params=pltpu.CompilerParams(
            collective_id=0, has_side_effects=True, vmem_limit_bytes=56 * 1024 * 1024
        ),
    )(vectors, momenta, diagrams.T)
    return meson, values.T


def solution(mesh):
    return jax.shard_map(
        per_device,
        mesh=mesh,
        in_specs=(P("cuts", None, None, "space"), P(), P()),
        out_specs=(P("cuts", "space", None), P()),
        check_vma=False,
    )
```

```python
import functools
import math

import jax
import jax.numpy as jnp
from jax import lax
from jax.experimental import pallas as pl
from jax.experimental.pallas import tpu as pltpu
from jax.sharding import PartitionSpec as P

TILE = 256
PHASES = 3
EXTENT = 96
RINGS = (12, 8, 2)
CUTS = 4
SUBS = 2
HOP_Z, HOP_Y, ROUND = 2.6, 3.9, 4.0
RELAY = 3

full_turn = 2.0 * math.pi
MESH = pl.DeviceIdType.MESH


def contract(left, right):
    return lax.dot_general(
        left, right, (((1,), (1,)), ((), ())), preferred_element_type=jnp.float32
    )


def halves(value):
    high = value.astype(jnp.bfloat16)
    low = (value - high.astype(jnp.float32)).astype(jnp.bfloat16)
    return high, low


def meet(extent):
    return extent // 2, extent - 1 - extent // 2


def far_first(extent):
    return sorted(range(1, extent), key=lambda k: -min(k, extent - k))


def relays(extent):
    by_relay, straight = [], []
    for side, count in enumerate(meet(extent)):
        for distance in range(1, count + 1):
            (by_relay if distance > RELAY else straight).append((side, distance))
    return by_relay, straight


def kernel(
    vec_hbm,
    mom_ref,
    dia_ref,
    meson_ref,
    value_ref,
    vec_ref,
    left,
    right,
    a0,
    a1,
    b0,
    b1,
    own_a,
    own_b,
    in_c,
    relay_d,
    in_d,
    piece,
    got,
    whole,
    total,
    sum_y,
    sum_x,
    sum_z,
    load_sem,
    send_a,
    recv_a,
    send_b,
    recv_b,
    send_c,
    recv_c,
    send_d,
    recv_relay,
    recv_d,
    send_e,
    recv_e,
    send_whole,
    recv_whole,
    send_y,
    recv_y,
    send_x,
    recv_x,
    send_z,
    recv_z,
):
    nz, ny, nx = RINGS
    nc = CUTS
    modes, sites = vec_ref.shape[1:]
    width = modes // SUBS
    rows_y = left.shape[2]
    rows_z = ny * rows_y
    rows_x = rows_y // nx
    quarter = modes // nc
    space = lax.axis_index("space")
    cut = lax.axis_index("cuts")
    x = lax.rem(space, nx)
    y = lax.rem(space // nx, ny)
    z = space // (nx * ny)
    sign = 1 - 2 * lax.rem(cut, 2)

    def at(zz, yy, xx, cc):
        return ((zz * ny + yy) * nx + xx, cc)

    def z_at(step):
        return lax.rem(z + step + 2 * nz, nz)

    def y_at(step):
        return lax.rem(y + step + 2 * ny, ny)

    load = pltpu.make_async_copy(vec_hbm.at[0], vec_ref, load_sem)
    load.start()

    peers = [at(z_at(k), y, x, cut) for k in sorted({1, nz - 1})]
    peers += [at(z, y_at(k), x, cut) for k in sorted({1, ny - 1})]
    others = [
        (lax.rem(x + dx, nx), lax.rem(cut + dc, nc), dx, dc)
        for dx in reversed(range(nx))
        for dc in (2, 1, 3, 0)
        if dx or dc
    ]
    peers += [at(z, y, xx, cc) for xx, cc, _, _ in others]
    barrier = pltpu.get_barrier_semaphore()
    for peer in peers:
        pl.semaphore_signal(barrier, inc=1, device_id=peer, device_id_type=MESH)

    load.wait()
    real_vec = vec_ref[0]
    imag_vec = vec_ref[1]
    depth = 2 * sites
    rh, rl = halves(real_vec)
    ih, il = halves(imag_vec)
    for part, (first, second) in enumerate((((rh, rl), (-ih, -il)), ((ih, il), (rh, rl)))):
        rows = slice(part * modes, (part + 1) * modes)
        for place, (high, low) in enumerate((first, second)):
            cols = place * sites
            right[rows, cols : cols + sites] = high
            right[rows, depth + cols : depth + cols + sites] = high
            right[rows, 2 * depth + cols : 2 * depth + cols + sites] = low

    lane = lax.broadcasted_iota(jnp.int32, (1, sites), 1)
    site = (space * sites + lane).astype(jnp.float32)
    line = jnp.floor((site + 0.5) * (1.0 / EXTENT))
    coord_x = site - line * EXTENT
    coord_z = jnp.floor((line + 0.5) * (1.0 / EXTENT))
    coord_y = line - coord_z * EXTENT
    blocks = modes // rows_y
    for phase in range(PHASES):
        dotted = (
            mom_ref[phase, 0].astype(jnp.float32) * coord_x
            + mom_ref[phase, 1].astype(jnp.float32) * coord_y
            + mom_ref[phase, 2].astype(jnp.float32) * coord_z
        )
        turned = dotted - jnp.floor((dotted + 0.5) * (1.0 / EXTENT)) * EXTENT
        angle = turned * (full_turn / EXTENT)
        cosine = jnp.cos(angle)
        sine = jnp.sin(angle)
        for place, value in enumerate(
            (real_vec * cosine + imag_vec * sine, real_vec * sine - imag_vec * cosine)
        ):
            high, low = halves(value)
            cols = place * sites
            for block in range(blocks):
                zz, yy = divmod(phase * blocks + block, ny)
                rows = slice(block * rows_y, (block + 1) * rows_y)
                left[zz, yy, :, cols : cols + sites] = high[rows]
                left[zz, yy, :, depth + cols : depth + cols + sites] = low[rows]
                left[zz, yy, :, 2 * depth + cols : 2 * depth + cols + sites] = high[rows]

    sends = []

    def post(source, target, send_sem, recv_sem, peer):
        copy = pltpu.make_async_remote_copy(
            src_ref=source,
            dst_ref=target,
            send_sem=send_sem,
            recv_sem=recv_sem,
            device_id=peer,
            device_id_type=MESH,
        )
        copy.start()
        sends.append(copy)

    def arrived(target, send_sem, recv_sem):
        pltpu.make_async_remote_copy(
            src_ref=target,
            dst_ref=target,
            send_sem=send_sem,
            recv_sem=recv_sem,
            device_id=at(z, y, x, cut),
            device_id_type=MESH,
        ).wait_recv()

    def local_a(spots, sub):
        rows = [left[zz].reshape(rows_z, left.shape[3]) for zz in spots]
        made = contract(jnp.concatenate(rows, axis=0), right[sub * width : (sub + 1) * width, :])
        return [made[k * rows_z : (k + 1) * rows_z] for k in range(len(spots))]

    def local_b(spots, sub):
        high = nz * rows_y
        rows = [left[:, yy].reshape(high, left.shape[3]) for yy in spots]
        start = modes + sub * width
        made = contract(jnp.concatenate(rows, axis=0), right[start : start + width, :])
        return [made[k * high : (k + 1) * high] for k in range(len(spots))]

    def ring(hops, slots, own, send_sems, recv_sems, sub, local, finish, step_at, peer_of, tick):
        def hop(step):
            ways = [(0, sign)] + ([(1, -sign)] if step < hops[1] else [])
            spots = [step_at(way * (hops[direction] - step)) for direction, way in ways]
            if step == hops[1]:
                spots.append(step_at(0))
            made = local(spots, sub)
            for (direction, way), mine in zip(ways, made):
                here = slots[direction].at[step, sub]
                if step:
                    arrived(here, send_sems.at[direction, step - 1, sub], recv_sems.at[direction, step - 1, sub])
                    here[...] += mine
                else:
                    here[...] = mine
                post(
                    here,
                    slots[direction].at[step + 1, sub],
                    send_sems.at[direction, step, sub],
                    recv_sems.at[direction, step, sub],
                    peer_of(way),
                )
            if step == hops[1]:
                own[sub] = made[1].reshape(own.shape[1:])

        def last():
            value = own[sub].reshape(slots[0].shape[2:]) if hops[0] > hops[1] else local([step_at(0)], sub)[0]
            for direction in (1, 0):
                count = hops[direction]
                if count:
                    here = slots[direction].at[count, sub]
                    arrived(here, send_sems.at[direction, count - 1, sub], recv_sems.at[direction, count - 1, sub])
                    value += here[...]
            finish(sub, value)

        made = [(tick * (step * SUBS + sub), functools.partial(hop, step)) for step in range(hops[0])]
        made.append((tick * (hops[0] * SUBS + sub), last))
        return made

    def z_peer(way):
        return at(z_at(way), y, x, cut)

    def y_peer(way):
        return at(z, y_at(way), x, cut)

    def way_of(side):
        return sign if side == 0 else -sign

    hops_z, hops_y = meet(nz), meet(ny)
    per = width // quarter

    def keep(part, sub, value):
        for xx in range(nx):
            for k in range(per):
                piece[xx, sub * per + k, part] = value[
                    xx * rows_x : (xx + 1) * rows_x, k * quarter : (k + 1) * quarter
                ]

    def spread_a(sub, value):
        own_a[sub] = value.reshape(ny, rows_y, width)
        for k in far_first(ny):
            post(
                own_a.at[sub, y_at(k)], in_c.at[sub, k - 1], send_c.at[sub, k - 1], recv_c.at[sub, k - 1], y_peer(k)
            )

    def gather_a(sub):
        value = own_a[sub, y]
        for k in far_first(ny)[::-1]:
            arrived(in_c.at[sub, k - 1], send_c.at[sub, k - 1], recv_c.at[sub, k - 1])
            value += in_c[sub, k - 1]
        keep(0, sub, value)

    by_relay, straight = relays(nz)

    def spread_b(sub, value):
        own_b[sub] = value.reshape(nz, rows_y, width)
        for k, (side, distance) in sorted(enumerate(by_relay), key=lambda item: -item[1][1]):
            way = way_of(side)
            post(
                own_b.at[sub, z_at(-way * distance)],
                relay_d.at[sub, k],
                send_d.at[sub, k],
                recv_relay.at[sub, k],
                z_peer(-way * (distance - RELAY)),
            )
        for k, (side, distance) in sorted(enumerate(straight), key=lambda item: -item[1][1]):
            if not has_relay(side, distance):
                send_straight(sub, k, side, distance)

    def has_relay(side, distance):
        return distance == RELAY and any(other == side for other, _ in by_relay)

    def send_straight(sub, k, side, distance):
        way = way_of(side)
        post(
            own_b.at[sub, z_at(-way * distance)],
            in_d.at[sub, k],
            send_d.at[sub, len(by_relay) + k],
            recv_d.at[sub, k],
            z_peer(-way * distance),
        )

    def relay_b(sub):
        for k, (side, distance) in enumerate(straight):
            if has_relay(side, distance):
                spot = z_at(-way_of(side) * distance)
                value = own_b[sub, spot]
                for j, (other, _) in enumerate(by_relay):
                    if other == side:
                        arrived(relay_d.at[sub, j], send_d.at[sub, j], recv_relay.at[sub, j])
                        value += relay_d[sub, j]
                own_b[sub, spot] = value
                send_straight(sub, k, side, distance)

    def gather_b(sub):
        value = own_b[sub, z]
        for k, (side, distance) in enumerate(straight):
            arrived(in_d.at[sub, k], send_d.at[sub, len(by_relay) + k], recv_d.at[sub, k])
            value += in_d[sub, k]
        keep(1, sub, value)

    events = []
    for sub in range(SUBS):
        events += ring(hops_y, (b0, b1), own_b, send_b, recv_b, sub, local_b, spread_b, y_at, y_peer, HOP_Y)
        end = events[-1][0]
        events.append((end + ROUND, functools.partial(relay_b, sub)))
        events.append((end + 2 * ROUND, functools.partial(gather_b, sub)))
        events += ring(hops_z, (a0, a1), own_a, send_a, recv_a, sub, local_a, spread_a, z_at, z_peer, HOP_Z)
        events[-1] = (end + 0.1, events[-1][1])
        events.append((end + 1.5 * ROUND, functools.partial(gather_a, sub)))

    pl.semaphore_wait(barrier, len(peers))
    for _, event in sorted(events, key=lambda pair: pair[0]):
        event()

    for xx, cc, dx, dc in others:
        post(piece.at[xx, cc], got.at[dx, dc], send_e.at[dx, dc], recv_e.at[dx, dc], at(z, y, xx, cc))
    for dx in range(1, nx):
        xx = lax.rem(x + dx, nx)
        post(piece.at[xx], whole.at[dx], send_whole.at[dx], recv_whole.at[dx], at(z, y, xx, cut))

    entries = dia_ref.shape[1]
    lanes = sum_y.shape[2]
    tile_id = dia_ref[0:1, :]
    code = (
        (dia_ref[3:4, :] * 2 + (tile_id >> 1)) * (nc * nc)
        + dia_ref[1:2, :] * nc
        + dia_ref[2:3, :]
        + (tile_id & 1) * lanes
    ).astype(jnp.float32)
    eye = lax.broadcasted_iota(jnp.int32, (entries, entries), 0) == lax.broadcasted_iota(
        jnp.int32, (entries, entries), 1
    )
    code = jnp.sum(jnp.where(eye, code, 0.0), axis=1, keepdims=True)
    lane_code = lax.broadcasted_iota(jnp.int32, (entries, lanes), 1).astype(jnp.float32)
    pick = [lane_code + float(b * lanes) == code for b in range(2)]

    for dc in range(nc):
        for dx in range(nx):
            if dx or dc:
                arrived(got.at[dx, dc], send_e.at[dx, dc], recv_e.at[dx, dc])
        value = got[0, dc] if dc else piece[x, cut]
        for dx in range(1, nx):
            value += got[dx, dc]
        total[lax.rem(cut - dc + nc, nc)] = value

    re = [total[t, 0] for t in range(nc)]
    im = [total[t, 1] for t in range(nc)]

    def down(value):
        return jnp.sum(value, axis=0, keepdims=True)

    rr, ii = {}, {}
    for s in range(nc):
        for t in range(s, nc):
            rr[s, t] = rr[t, s] = down(re[s] * re[t] + im[s] * im[t])
            if s == t:
                ii[s, t] = jnp.zeros_like(rr[s, t])
            else:
                ii[s, t] = down(im[s] * re[t] - re[s] * im[t])
                ii[t, s] = -ii[s, t]
    pairs = [(s, t) for s in range(nc) for t in range(nc)]
    key = z // (nz // (2 * PHASES))
    own_b_col = cut // 2
    lane_id = lax.broadcasted_iota(jnp.int32, (nc * nc, lanes), 1)
    row_id = lax.broadcasted_iota(jnp.int32, (nc * nc, lanes), 0)
    spot = lane_id == key * (nc * nc) + row_id
    tile_rows = lax.broadcasted_iota(jnp.int32, sum_y.shape[1:], 0)
    table = jnp.zeros(sum_y.shape[1:], jnp.float32)
    for part, values in enumerate((rr, ii)):
        column = jnp.sum(jnp.concatenate([values[p] for p in pairs], axis=0), axis=1, keepdims=True)
        lane_row = down(jnp.where(spot, column, 0.0))
        table = jnp.where(tile_rows == 2 * part + own_b_col, lane_row, table)

    def all_sum(table, slots, send_sems, recv_sems, me, count, targets):
        slots[me] = table
        for k, peer in enumerate(targets):
            post(slots.at[me], slots.at[me], send_sems.at[k], recv_sems.at[me], peer)
        for k in range(1, count):
            source = lax.rem(me + k, count)
            arrived(slots.at[source], send_sems.at[k - 1], recv_sems.at[source])
        value = slots[0]
        for k in range(1, count):
            value += slots[k]
        return value

    table = all_sum(table, sum_y, send_y, recv_y, y, ny, [at(z, y_at(k), x, cut) for k in far_first(ny)])

    rows_own = piece[x]
    for dx in range(1, nx):
        arrived(whole.at[dx], send_whole.at[dx], recv_whole.at[dx])
        rows_own += whole[dx]
    for part in range(2):
        for k in range(nc):
            start = part * modes + k * quarter
            meson_ref[0, :, start : start + quarter] = rows_own[k, part]

    table = all_sum(
        table, sum_x, send_x, recv_x, x * nc + cut, nx * nc, [at(z, y, xx, cc) for xx, cc, _, _ in others]
    )
    table = all_sum(table, sum_z, send_z, recv_z, z, nz, [at(z_at(k), y, x, cut) for k in far_first(nz)])

    for part in range(2):
        value = jnp.where(pick[0], table[2 * part : 2 * part + 1], 0.0) + jnp.where(
            pick[1], table[2 * part + 1 : 2 * part + 2], 0.0
        )
        column = jnp.sum(value, axis=1, keepdims=True)
        value_ref[part : part + 1, :] = down(jnp.where(eye, column, 0.0)) / TILE

    for copy in sends:
        copy.wait_send()


def per_device(vectors, momenta, diagrams):
    nz, ny, nx = RINGS
    modes, sites = vectors.shape[2:]
    rows = PHASES * modes
    rows_y = rows // (nz * ny)
    rows_z = rows_y * ny
    width = modes // SUBS
    quarter = modes // CUTS
    lanes = max(128, 2 * PHASES * CUTS * CUTS)
    depth = 6 * sites
    z_hops, y_hops = meet(nz), meet(ny)
    by_relay, straight = relays(nz)
    f32, bf16 = jnp.float32, jnp.bfloat16
    dma = pltpu.SemaphoreType.DMA

    def slots(hops, *shape):
        return [pltpu.VMEM((count + 1, SUBS, *shape), f32) for count in hops]

    def sems(hops):
        return [dma((2, hops[0], SUBS))] * 2

    scratch = [
        pltpu.VMEM(vectors.shape[1:], f32),
        pltpu.VMEM((nz, ny, rows_y, depth), bf16),
        pltpu.VMEM((2 * modes, depth), bf16),
        *slots(z_hops, rows_z, width),
        *slots(y_hops, nz * rows_y, width),
        pltpu.VMEM((SUBS, ny, rows_y, width), f32),
        pltpu.VMEM((SUBS, nz, rows_y, width), f32),
        pltpu.VMEM((SUBS, ny - 1, rows_y, width), f32),
        pltpu.VMEM((SUBS, max(1, len(by_relay)), rows_y, width), f32),
        pltpu.VMEM((SUBS, len(straight), rows_y, width), f32),
        pltpu.VMEM((nx, CUTS, 2, rows_y // nx, quarter), f32),
        pltpu.VMEM((nx, CUTS, 2, rows_y // nx, quarter), f32),
        pltpu.VMEM((nx, CUTS, 2, rows_y // nx, quarter), f32),
        pltpu.VMEM((CUTS, 2, rows_y // nx, quarter), f32),
        pltpu.VMEM((ny, 8, lanes), f32),
        pltpu.VMEM((nx * CUTS, 8, lanes), f32),
        pltpu.VMEM((nz, 8, lanes), f32),
        dma,
        *sems(z_hops),
        *sems(y_hops),
        *[dma((SUBS, ny - 1))] * 2,
        dma((SUBS, nz - 1)),
        dma((SUBS, max(1, len(by_relay)))),
        dma((SUBS, len(straight))),
        *[dma((nx, CUTS))] * 2,
        *[dma((nx,))] * 2,
        *[dma((ny,))] * 2,
        *[dma((nx * CUTS,))] * 2,
        *[dma((nz,))] * 2,
    ]
    vmem = pl.BlockSpec(memory_space=pltpu.VMEM)
    meson, values = pl.pallas_call(
        kernel,
        out_shape=(
            jax.ShapeDtypeStruct((1, rows_y // nx, 2 * modes), f32),
            jax.ShapeDtypeStruct((2, diagrams.shape[0]), f32),
        ),
        in_specs=[pl.BlockSpec(memory_space=pl.ANY), pl.BlockSpec(memory_space=pltpu.SMEM), vmem],
        out_specs=(vmem, vmem),
        scratch_shapes=scratch,
        compiler_params=pltpu.CompilerParams(
            collective_id=0, has_side_effects=True, vmem_limit_bytes=56 * 1024 * 1024
        ),
    )(vectors, momenta, diagrams.T)
    return meson, values.T


def solution(mesh):
    return jax.shard_map(
        per_device,
        mesh=mesh,
        in_specs=(P("cuts", None, None, "space"), P(), P()),
        out_specs=(P("cuts", "space", None), P()),
        check_vma=False,
    )
```

```python
import functools
import math

import jax
import jax.numpy as jnp
from jax import lax
from jax.experimental import pallas as pl
from jax.experimental.pallas import tpu as pltpu
from jax.sharding import PartitionSpec as P

TILE = 256
PHASES = 3
EXTENT = 96
RINGS = (12, 8, 2)
CUTS = 4
SUBS = 2
HOP_Z, HOP_Y, ROUND = 2.6, 3.9, 4.0
RELAY = 3

full_turn = 2.0 * math.pi
MESH = pl.DeviceIdType.MESH


def contract(left, right):
    return lax.dot_general(
        left, right, (((1,), (1,)), ((), ())), preferred_element_type=jnp.float32
    )


def halves(value):
    high = value.astype(jnp.bfloat16)
    low = (value - high.astype(jnp.float32)).astype(jnp.bfloat16)
    return high, low


def meet(extent):
    return extent // 2, extent - 1 - extent // 2


def far_first(extent):
    return sorted(range(1, extent), key=lambda k: -min(k, extent - k))


def relays(extent):
    by_relay, straight = [], []
    for side, count in enumerate(meet(extent)):
        for distance in range(1, count + 1):
            (by_relay if distance > RELAY else straight).append((side, distance))
    return by_relay, straight


def kernel(
    vec_hbm,
    mom_ref,
    dia_ref,
    meson_ref,
    value_ref,
    vec_ref,
    left,
    right,
    a0,
    a1,
    b0,
    b1,
    own_a,
    own_b,
    in_c,
    relay_d,
    in_d,
    piece,
    got,
    whole,
    total,
    sum_y,
    sum_x,
    sum_z,
    load_sem,
    send_a,
    recv_a,
    send_b,
    recv_b,
    send_c,
    recv_c,
    send_d,
    recv_relay,
    recv_d,
    send_e,
    recv_e,
    send_whole,
    recv_whole,
    send_y,
    recv_y,
    send_x,
    recv_x,
    send_z,
    recv_z,
):
    nz, ny, nx = RINGS
    nc = CUTS
    modes, sites = vec_ref.shape[1:]
    width = modes // SUBS
    rows_y = left.shape[2]
    rows_z = ny * rows_y
    rows_x = rows_y // nx
    quarter = modes // nc
    space = lax.axis_index("space")
    cut = lax.axis_index("cuts")
    x = lax.rem(space, nx)
    y = lax.rem(space // nx, ny)
    z = space // (nx * ny)
    sign = 1 - 2 * lax.rem(cut, 2)

    def at(zz, yy, xx, cc):
        return ((zz * ny + yy) * nx + xx, cc)

    def z_at(step):
        return lax.rem(z + step + 2 * nz, nz)

    def y_at(step):
        return lax.rem(y + step + 2 * ny, ny)

    load = pltpu.make_async_copy(vec_hbm.at[0], vec_ref, load_sem)
    load.start()

    peers = [at(z_at(k), y, x, cut) for k in sorted({1, nz - 1})]
    peers += [at(z, y_at(k), x, cut) for k in sorted({1, ny - 1})]
    others = [
        (lax.rem(x + dx, nx), lax.rem(cut + dc, nc), dx, dc)
        for dx in reversed(range(nx))
        for dc in (2, 1, 3, 0)
        if dx or dc
    ]
    peers += [at(z, y, xx, cc) for xx, cc, _, _ in others]
    barrier = pltpu.get_barrier_semaphore()
    for peer in peers:
        pl.semaphore_signal(barrier, inc=1, device_id=peer, device_id_type=MESH)

    load.wait()
    real_vec = vec_ref[0]
    imag_vec = vec_ref[1]
    depth = 2 * sites
    rh, rl = halves(real_vec)
    ih, il = halves(imag_vec)
    for part, (first, second) in enumerate((((rh, rl), (-ih, -il)), ((ih, il), (rh, rl)))):
        rows = slice(part * modes, (part + 1) * modes)
        for place, (high, low) in enumerate((first, second)):
            cols = place * sites
            right[rows, cols : cols + sites] = high
            right[rows, depth + cols : depth + cols + sites] = high
            right[rows, 2 * depth + cols : 2 * depth + cols + sites] = low

    lane = lax.broadcasted_iota(jnp.int32, (1, sites), 1)
    site = (space * sites + lane).astype(jnp.float32)
    line = jnp.floor((site + 0.5) * (1.0 / EXTENT))
    coord_x = site - line * EXTENT
    coord_z = jnp.floor((line + 0.5) * (1.0 / EXTENT))
    coord_y = line - coord_z * EXTENT
    blocks = modes // rows_y
    for phase in range(PHASES):
        dotted = (
            mom_ref[phase, 0].astype(jnp.float32) * coord_x
            + mom_ref[phase, 1].astype(jnp.float32) * coord_y
            + mom_ref[phase, 2].astype(jnp.float32) * coord_z
        )
        turned = dotted - jnp.floor((dotted + 0.5) * (1.0 / EXTENT)) * EXTENT
        angle = turned * (full_turn / EXTENT)
        cosine = jnp.cos(angle)
        sine = jnp.sin(angle)
        for place, value in enumerate(
            (real_vec * cosine + imag_vec * sine, real_vec * sine - imag_vec * cosine)
        ):
            high, low = halves(value)
            cols = place * sites
            for block in range(blocks):
                zz, yy = divmod(phase * blocks + block, ny)
                rows = slice(block * rows_y, (block + 1) * rows_y)
                left[zz, yy, :, cols : cols + sites] = high[rows]
                left[zz, yy, :, depth + cols : depth + cols + sites] = low[rows]
                left[zz, yy, :, 2 * depth + cols : 2 * depth + cols + sites] = high[rows]

    sends = []

    def post(source, target, send_sem, recv_sem, peer):
        copy = pltpu.make_async_remote_copy(
            src_ref=source,
            dst_ref=target,
            send_sem=send_sem,
            recv_sem=recv_sem,
            device_id=peer,
            device_id_type=MESH,
        )
        copy.start()
        sends.append(copy)

    def arrived(target, send_sem, recv_sem):
        pltpu.make_async_remote_copy(
            src_ref=target,
            dst_ref=target,
            send_sem=send_sem,
            recv_sem=recv_sem,
            device_id=at(z, y, x, cut),
            device_id_type=MESH,
        ).wait_recv()

    def local_a(spots, sub):
        rows = [left[zz].reshape(rows_z, left.shape[3]) for zz in spots]
        made = contract(jnp.concatenate(rows, axis=0), right[sub * width : (sub + 1) * width, :])
        return [made[k * rows_z : (k + 1) * rows_z] for k in range(len(spots))]

    def local_b(spots, sub):
        high = nz * rows_y
        rows = [left[:, yy].reshape(high, left.shape[3]) for yy in spots]
        start = modes + sub * width
        made = contract(jnp.concatenate(rows, axis=0), right[start : start + width, :])
        return [made[k * high : (k + 1) * high] for k in range(len(spots))]

    def ring(hops, slots, own, send_sems, recv_sems, sub, local, finish, step_at, peer_of, tick):
        def hop(step):
            ways = [(0, sign)] + ([(1, -sign)] if step < hops[1] else [])
            spots = [step_at(way * (hops[direction] - step)) for direction, way in ways]
            if step == hops[1]:
                spots.append(step_at(0))
            made = local(spots, sub)
            for (direction, way), mine in zip(ways, made):
                here = slots[direction].at[step, sub]
                if step:
                    arrived(here, send_sems.at[direction, step - 1, sub], recv_sems.at[direction, step - 1, sub])
                    here[...] += mine
                else:
                    here[...] = mine
                post(
                    here,
                    slots[direction].at[step + 1, sub],
                    send_sems.at[direction, step, sub],
                    recv_sems.at[direction, step, sub],
                    peer_of(way),
                )
            if step == hops[1]:
                own[sub] = made[1].reshape(own.shape[1:])

        def last():
            value = own[sub].reshape(slots[0].shape[2:]) if hops[0] > hops[1] else local([step_at(0)], sub)[0]
            for direction in (1, 0):
                count = hops[direction]
                if count:
                    here = slots[direction].at[count, sub]
                    arrived(here, send_sems.at[direction, count - 1, sub], recv_sems.at[direction, count - 1, sub])
                    value += here[...]
            finish(sub, value)

        made = [(tick * (step * SUBS + sub), functools.partial(hop, step)) for step in range(hops[0])]
        made.append((tick * (hops[0] * SUBS + sub), last))
        return made

    def z_peer(way):
        return at(z_at(way), y, x, cut)

    def y_peer(way):
        return at(z, y_at(way), x, cut)

    def way_of(side):
        return sign if side == 0 else -sign

    hops_z, hops_y = meet(nz), meet(ny)
    per = width // quarter

    def keep(part, sub, value):
        for xx in range(nx):
            for k in range(per):
                piece[xx, sub * per + k, part] = value[
                    xx * rows_x : (xx + 1) * rows_x, k * quarter : (k + 1) * quarter
                ]

    def spread_a(sub, value):
        own_a[sub] = value.reshape(ny, rows_y, width)
        for k in far_first(ny):
            post(
                own_a.at[sub, y_at(k)], in_c.at[sub, k - 1], send_c.at[sub, k - 1], recv_c.at[sub, k - 1], y_peer(k)
            )

    def gather_a(sub):
        value = own_a[sub, y]
        for k in far_first(ny)[::-1]:
            arrived(in_c.at[sub, k - 1], send_c.at[sub, k - 1], recv_c.at[sub, k - 1])
            value += in_c[sub, k - 1]
        keep(0, sub, value)

    by_relay, straight = relays(nz)

    def spread_b(sub, value):
        own_b[sub] = value.reshape(nz, rows_y, width)
        for k, (side, distance) in sorted(enumerate(by_relay), key=lambda item: -item[1][1]):
            way = way_of(side)
            post(
                own_b.at[sub, z_at(-way * distance)],
                relay_d.at[sub, k],
                send_d.at[sub, k],
                recv_relay.at[sub, k],
                z_peer(-way * (distance - RELAY)),
            )
        for k, (side, distance) in sorted(enumerate(straight), key=lambda item: -item[1][1]):
            if not has_relay(side, distance):
                send_straight(sub, k, side, distance)

    def has_relay(side, distance):
        return distance == RELAY and any(other == side for other, _ in by_relay)

    def send_straight(sub, k, side, distance):
        way = way_of(side)
        post(
            own_b.at[sub, z_at(-way * distance)],
            in_d.at[sub, k],
            send_d.at[sub, len(by_relay) + k],
            recv_d.at[sub, k],
            z_peer(-way * distance),
        )

    def relay_b(sub):
        for k, (side, distance) in enumerate(straight):
            if has_relay(side, distance):
                spot = z_at(-way_of(side) * distance)
                value = own_b[sub, spot]
                for j, (other, _) in enumerate(by_relay):
                    if other == side:
                        arrived(relay_d.at[sub, j], send_d.at[sub, j], recv_relay.at[sub, j])
                        value += relay_d[sub, j]
                own_b[sub, spot] = value
                send_straight(sub, k, side, distance)

    def gather_b(sub):
        value = own_b[sub, z]
        for k, (side, distance) in enumerate(straight):
            arrived(in_d.at[sub, k], send_d.at[sub, len(by_relay) + k], recv_d.at[sub, k])
            value += in_d[sub, k]
        keep(1, sub, value)

    events = []
    for sub in range(SUBS):
        events += ring(hops_y, (b0, b1), own_b, send_b, recv_b, sub, local_b, spread_b, y_at, y_peer, HOP_Y)
        end = events[-1][0]
        events.append((end + ROUND, functools.partial(relay_b, sub)))
        events.append((end + 2 * ROUND, functools.partial(gather_b, sub)))
        events += ring(hops_z, (a0, a1), own_a, send_a, recv_a, sub, local_a, spread_a, z_at, z_peer, HOP_Z)
        events[-1] = (end + 0.1, events[-1][1])
        events.append((end + 1.5 * ROUND, functools.partial(gather_a, sub)))

    pl.semaphore_wait(barrier, len(peers))
    for _, event in sorted(events, key=lambda pair: pair[0]):
        event()

    for xx, cc, dx, dc in others:
        post(piece.at[xx, cc], got.at[dx, dc], send_e.at[dx, dc], recv_e.at[dx, dc], at(z, y, xx, cc))
    for dx in range(1, nx):
        xx = lax.rem(x + dx, nx)
        post(piece.at[xx], whole.at[dx], send_whole.at[dx], recv_whole.at[dx], at(z, y, xx, cut))

    entries = dia_ref.shape[1]
    lanes = sum_y.shape[2]
    tile_id = dia_ref[0:1, :]
    code = (
        (dia_ref[3:4, :] * 2 + (tile_id >> 1)) * (nc * nc)
        + dia_ref[1:2, :] * nc
        + dia_ref[2:3, :]
        + (tile_id & 1) * lanes
    ).astype(jnp.float32)
    eye = lax.broadcasted_iota(jnp.int32, (entries, entries), 0) == lax.broadcasted_iota(
        jnp.int32, (entries, entries), 1
    )
    code = jnp.sum(jnp.where(eye, code, 0.0), axis=1, keepdims=True)
    lane_code = lax.broadcasted_iota(jnp.int32, (entries, lanes), 1).astype(jnp.float32)
    pick = [lane_code + float(b * lanes) == code for b in range(2)]

    for dc in range(nc):
        for dx in range(nx):
            if dx or dc:
                arrived(got.at[dx, dc], send_e.at[dx, dc], recv_e.at[dx, dc])
        value = got[0, dc] if dc else piece[x, cut]
        for dx in range(1, nx):
            value += got[dx, dc]
        total[lax.rem(cut - dc + nc, nc)] = value

    re = [total[t, 0] for t in range(nc)]
    im = [total[t, 1] for t in range(nc)]

    def down(value):
        return jnp.sum(value, axis=0, keepdims=True)

    rr, ii = {}, {}
    for s in range(nc):
        for t in range(s, nc):
            rr[s, t] = rr[t, s] = down(re[s] * re[t] + im[s] * im[t])
            if s == t:
                ii[s, t] = jnp.zeros_like(rr[s, t])
            else:
                ii[s, t] = down(im[s] * re[t] - re[s] * im[t])
                ii[t, s] = -ii[s, t]
    pairs = [(s, t) for s in range(nc) for t in range(nc)]
    key = z // (nz // (2 * PHASES))
    own_b_col = cut // 2
    lane_id = lax.broadcasted_iota(jnp.int32, (nc * nc, lanes), 1)
    row_id = lax.broadcasted_iota(jnp.int32, (nc * nc, lanes), 0)
    spot = lane_id == key * (nc * nc) + row_id
    tile_rows = lax.broadcasted_iota(jnp.int32, sum_y.shape[1:], 0)
    table = jnp.zeros(sum_y.shape[1:], jnp.float32)
    for part, values in enumerate((rr, ii)):
        column = jnp.sum(jnp.concatenate([values[p] for p in pairs], axis=0), axis=1, keepdims=True)
        lane_row = down(jnp.where(spot, column, 0.0))
        table = jnp.where(tile_rows == 2 * part + own_b_col, lane_row, table)

    def all_sum(table, slots, send_sems, recv_sems, me, count, targets):
        slots[me] = table
        for k, peer in enumerate(targets):
            post(slots.at[me], slots.at[me], send_sems.at[k], recv_sems.at[me], peer)
        for k in range(1, count):
            source = lax.rem(me + k, count)
            arrived(slots.at[source], send_sems.at[k - 1], recv_sems.at[source])
        value = slots[0]
        for k in range(1, count):
            value += slots[k]
        return value

    table = all_sum(table, sum_y, send_y, recv_y, y, ny, [at(z, y_at(k), x, cut) for k in far_first(ny)])

    rows_own = piece[x]
    for dx in range(1, nx):
        arrived(whole.at[dx], send_whole.at[dx], recv_whole.at[dx])
        rows_own += whole[dx]
    for part in range(2):
        for k in range(nc):
            start = part * modes + k * quarter
            meson_ref[0, :, start : start + quarter] = rows_own[k, part]

    table = all_sum(
        table, sum_x, send_x, recv_x, x * nc + cut, nx * nc, [at(z, y, xx, cc) for xx, cc, _, _ in others]
    )
    table = all_sum(table, sum_z, send_z, recv_z, z, nz, [at(z_at(k), y, x, cut) for k in far_first(nz)])

    for part in range(2):
        value = jnp.where(pick[0], table[2 * part : 2 * part + 1], 0.0) + jnp.where(
            pick[1], table[2 * part + 1 : 2 * part + 2], 0.0
        )
        column = jnp.sum(value, axis=1, keepdims=True)
        value_ref[part : part + 1, :] = down(jnp.where(eye, column, 0.0)) / TILE

    for copy in sends:
        copy.wait_send()


def per_device(vectors, momenta, diagrams):
    nz, ny, nx = RINGS
    modes, sites = vectors.shape[2:]
    rows = PHASES * modes
    rows_y = rows // (nz * ny)
    rows_z = rows_y * ny
    width = modes // SUBS
    quarter = modes // CUTS
    lanes = max(128, 2 * PHASES * CUTS * CUTS)
    depth = 6 * sites
    z_hops, y_hops = meet(nz), meet(ny)
    by_relay, straight = relays(nz)
    f32, bf16 = jnp.float32, jnp.bfloat16
    dma = pltpu.SemaphoreType.DMA

    def slots(hops, *shape):
        return [pltpu.VMEM((count + 1, SUBS, *shape), f32) for count in hops]

    def sems(hops):
        return [dma((2, hops[0], SUBS))] * 2

    scratch = [
        pltpu.VMEM(vectors.shape[1:], f32),
        pltpu.VMEM((nz, ny, rows_y, depth), bf16),
        pltpu.VMEM((2 * modes, depth), bf16),
        *slots(z_hops, rows_z, width),
        *slots(y_hops, nz * rows_y, width),
        pltpu.VMEM((SUBS, ny, rows_y, width), f32),
        pltpu.VMEM((SUBS, nz, rows_y, width), f32),
        pltpu.VMEM((SUBS, ny - 1, rows_y, width), f32),
        pltpu.VMEM((SUBS, max(1, len(by_relay)), rows_y, width), f32),
        pltpu.VMEM((SUBS, len(straight), rows_y, width), f32),
        pltpu.VMEM((nx, CUTS, 2, rows_y // nx, quarter), f32),
        pltpu.VMEM((nx, CUTS, 2, rows_y // nx, quarter), f32),
        pltpu.VMEM((nx, CUTS, 2, rows_y // nx, quarter), f32),
        pltpu.VMEM((CUTS, 2, rows_y // nx, quarter), f32),
        pltpu.VMEM((ny, 8, lanes), f32),
        pltpu.VMEM((nx * CUTS, 8, lanes), f32),
        pltpu.VMEM((nz, 8, lanes), f32),
        dma,
        *sems(z_hops),
        *sems(y_hops),
        *[dma((SUBS, ny - 1))] * 2,
        dma((SUBS, nz - 1)),
        dma((SUBS, max(1, len(by_relay)))),
        dma((SUBS, len(straight))),
        *[dma((nx, CUTS))] * 2,
        *[dma((nx,))] * 2,
        *[dma((ny,))] * 2,
        *[dma((nx * CUTS,))] * 2,
        *[dma((nz,))] * 2,
    ]
    vmem = pl.BlockSpec(memory_space=pltpu.VMEM)
    meson, values = pl.pallas_call(
        kernel,
        out_shape=(
            pltpu.VMEM((1, rows_y // nx, 2 * modes), f32),
            pltpu.VMEM((2, diagrams.shape[0]), f32),
        ),
        in_specs=[pl.BlockSpec(memory_space=pl.ANY), pl.BlockSpec(memory_space=pltpu.SMEM), vmem],
        out_specs=(vmem, vmem),
        scratch_shapes=scratch,
        compiler_params=pltpu.CompilerParams(
            collective_id=0, has_side_effects=True, vmem_limit_bytes=56 * 1024 * 1024
        ),
    )(vectors, momenta, diagrams.T)
    return meson, values.T


def solution(mesh):
    return jax.shard_map(
        per_device,
        mesh=mesh,
        in_specs=(P("cuts", None, None, "space"), P(), P()),
        out_specs=(P("cuts", "space", None), P()),
        check_vma=False,
    )
```

```python
import functools
import math

import jax
import jax.numpy as jnp
from jax import lax
from jax.experimental import pallas as pl
from jax.experimental.pallas import tpu as pltpu
from jax.sharding import PartitionSpec as P

TILE = 256
PHASES = 3
EXTENT = 96
RINGS = (12, 8, 2)
CUTS = 4
SUBS = 2
HOP_Z, HOP_Y, ROUND = 2.6, 3.9, 4.0
RELAY = 3

full_turn = 2.0 * math.pi
MESH = pl.DeviceIdType.MESH


def contract(left, right):
    return lax.dot_general(
        left, right, (((1,), (1,)), ((), ())), preferred_element_type=jnp.float32
    )


def halves(value):
    high = value.astype(jnp.bfloat16)
    low = (value - high.astype(jnp.float32)).astype(jnp.bfloat16)
    return high, low


def meet(extent):
    return extent // 2, extent - 1 - extent // 2


def far_first(extent):
    return sorted(range(1, extent), key=lambda k: -min(k, extent - k))


def relays(extent):
    by_relay, straight = [], []
    for side, count in enumerate(meet(extent)):
        for distance in range(1, count + 1):
            (by_relay if distance > RELAY else straight).append((side, distance))
    return by_relay, straight


def kernel(
    vec_hbm,
    mom_ref,
    dia_ref,
    meson_ref,
    value_ref,
    vec_ref,
    left,
    right,
    a0,
    a1,
    b0,
    b1,
    own_a,
    own_b,
    in_c,
    relay_d,
    in_d,
    piece,
    got,
    whole,
    total,
    sum_y,
    sum_x,
    sum_z,
    load_sem,
    send_a,
    recv_a,
    send_b,
    recv_b,
    send_c,
    recv_c,
    send_d,
    recv_relay,
    recv_d,
    send_e,
    recv_e,
    send_whole,
    recv_whole,
    send_y,
    recv_y,
    send_x,
    recv_x,
    send_z,
    recv_z,
):
    nz, ny, nx = RINGS
    nc = CUTS
    modes, sites = vec_ref.shape[1:]
    width = modes // SUBS
    rows_y = left.shape[2]
    rows_z = ny * rows_y
    rows_x = rows_y // nx
    quarter = modes // nc
    space = lax.axis_index("space")
    cut = lax.axis_index("cuts")
    x = lax.rem(space, nx)
    y = lax.rem(space // nx, ny)
    z = space // (nx * ny)
    sign = 1 - 2 * lax.rem(cut, 2)

    def at(zz, yy, xx, cc):
        return ((zz * ny + yy) * nx + xx, cc)

    def z_at(step):
        return lax.rem(z + step + 2 * nz, nz)

    def y_at(step):
        return lax.rem(y + step + 2 * ny, ny)

    load = pltpu.make_async_copy(vec_hbm.at[0], vec_ref, load_sem)
    load.start()

    peers = [at(z_at(k), y, x, cut) for k in sorted({1, nz - 1})]
    peers += [at(z, y_at(k), x, cut) for k in sorted({1, ny - 1})]
    others = [
        (lax.rem(x + dx, nx), lax.rem(cut + dc, nc), dx, dc)
        for dx in reversed(range(nx))
        for dc in (2, 1, 3, 0)
        if dx or dc
    ]
    peers += [at(z, y, xx, cc) for xx, cc, _, _ in others]
    barrier = pltpu.get_barrier_semaphore()
    for peer in peers:
        pl.semaphore_signal(barrier, inc=1, device_id=peer, device_id_type=MESH)

    load.wait()
    real_vec = vec_ref[0]
    imag_vec = vec_ref[1]
    depth = 2 * sites
    rh, rl = halves(real_vec)
    ih, il = halves(imag_vec)
    for part, (first, second) in enumerate((((rh, rl), (-ih, -il)), ((ih, il), (rh, rl)))):
        rows = slice(part * modes, (part + 1) * modes)
        for place, (high, low) in enumerate((first, second)):
            cols = place * sites
            right[rows, cols : cols + sites] = high
            right[rows, depth + cols : depth + cols + sites] = high
            right[rows, 2 * depth + cols : 2 * depth + cols + sites] = low

    lane = lax.broadcasted_iota(jnp.int32, (1, sites), 1)
    site = (space * sites + lane).astype(jnp.float32)
    line = jnp.floor((site + 0.5) * (1.0 / EXTENT))
    coord_x = site - line * EXTENT
    coord_z = jnp.floor((line + 0.5) * (1.0 / EXTENT))
    coord_y = line - coord_z * EXTENT
    blocks = modes // rows_y
    for phase in range(PHASES):
        dotted = (
            mom_ref[phase, 0].astype(jnp.float32) * coord_x
            + mom_ref[phase, 1].astype(jnp.float32) * coord_y
            + mom_ref[phase, 2].astype(jnp.float32) * coord_z
        )
        turned = dotted - jnp.floor((dotted + 0.5) * (1.0 / EXTENT)) * EXTENT
        angle = turned * (full_turn / EXTENT)
        cosine = jnp.cos(angle)
        sine = jnp.sin(angle)
        for place, value in enumerate(
            (real_vec * cosine + imag_vec * sine, real_vec * sine - imag_vec * cosine)
        ):
            high, low = halves(value)
            cols = place * sites
            for block in range(blocks):
                zz, yy = divmod(phase * blocks + block, ny)
                rows = slice(block * rows_y, (block + 1) * rows_y)
                left[zz, yy, :, cols : cols + sites] = high[rows]
                left[zz, yy, :, depth + cols : depth + cols + sites] = low[rows]
                left[zz, yy, :, 2 * depth + cols : 2 * depth + cols + sites] = high[rows]

    sends = []

    def post(source, target, send_sem, recv_sem, peer):
        copy = pltpu.make_async_remote_copy(
            src_ref=source,
            dst_ref=target,
            send_sem=send_sem,
            recv_sem=recv_sem,
            device_id=peer,
            device_id_type=MESH,
        )
        copy.start()
        sends.append(copy)

    def arrived(target, send_sem, recv_sem):
        pltpu.make_async_remote_copy(
            src_ref=target,
            dst_ref=target,
            send_sem=send_sem,
            recv_sem=recv_sem,
            device_id=at(z, y, x, cut),
            device_id_type=MESH,
        ).wait_recv()

    def local_a(spots, sub):
        rows = [left[zz].reshape(rows_z, left.shape[3]) for zz in spots]
        made = contract(jnp.concatenate(rows, axis=0), right[sub * width : (sub + 1) * width, :])
        return [made[k * rows_z : (k + 1) * rows_z] for k in range(len(spots))]

    def local_b(spots, sub):
        high = nz * rows_y
        rows = [left[:, yy].reshape(high, left.shape[3]) for yy in spots]
        start = modes + sub * width
        made = contract(jnp.concatenate(rows, axis=0), right[start : start + width, :])
        return [made[k * high : (k + 1) * high] for k in range(len(spots))]

    def ring(hops, slots, own, send_sems, recv_sems, sub, local, finish, step_at, peer_of, start, tick):
        def hop(step):
            ways = [(0, sign)] + ([(1, -sign)] if step < hops[1] else [])
            spots = [step_at(way * (hops[direction] - step)) for direction, way in ways]
            if step == hops[1]:
                spots.append(step_at(0))
            made = local(spots, sub)
            for (direction, way), mine in zip(ways, made):
                here = slots[direction].at[step, sub]
                if step:
                    arrived(here, send_sems.at[direction, step - 1, sub], recv_sems.at[direction, step - 1, sub])
                    here[...] += mine
                else:
                    here[...] = mine
                post(
                    here,
                    slots[direction].at[step + 1, sub],
                    send_sems.at[direction, step, sub],
                    recv_sems.at[direction, step, sub],
                    peer_of(way),
                )
            if step == hops[1]:
                own[sub] = made[1].reshape(own.shape[1:])

        def last():
            value = own[sub].reshape(slots[0].shape[2:]) if hops[0] > hops[1] else local([step_at(0)], sub)[0]
            for direction in (1, 0):
                count = hops[direction]
                if count:
                    here = slots[direction].at[count, sub]
                    arrived(here, send_sems.at[direction, count - 1, sub], recv_sems.at[direction, count - 1, sub])
                    value += here[...]
            finish(sub, value)

        made = [(start + tick * (step * SUBS + sub), functools.partial(hop, step)) for step in range(hops[0])]
        made.append((start + tick * (hops[0] * SUBS + sub), last))
        return made

    def z_peer(way):
        return at(z_at(way), y, x, cut)

    def y_peer(way):
        return at(z, y_at(way), x, cut)

    def way_of(side):
        return sign if side == 0 else -sign

    hops_z, hops_y = meet(nz), meet(ny)
    per = width // quarter

    def keep(part, sub, value):
        for xx in range(nx):
            for k in range(per):
                piece[xx, sub * per + k, part] = value[
                    xx * rows_x : (xx + 1) * rows_x, k * quarter : (k + 1) * quarter
                ]

    def spread_a(sub, value):
        own_a[sub] = value.reshape(ny, rows_y, width)
        for k in far_first(ny):
            post(
                own_a.at[sub, y_at(k)], in_c.at[sub, k - 1], send_c.at[sub, k - 1], recv_c.at[sub, k - 1], y_peer(k)
            )

    def gather_a(sub):
        value = own_a[sub, y]
        for k in far_first(ny)[::-1]:
            arrived(in_c.at[sub, k - 1], send_c.at[sub, k - 1], recv_c.at[sub, k - 1])
            value += in_c[sub, k - 1]
        keep(0, sub, value)

    by_relay, straight = relays(nz)

    def spread_b(sub, value):
        own_b[sub] = value.reshape(nz, rows_y, width)
        for k, (side, distance) in sorted(enumerate(by_relay), key=lambda item: -item[1][1]):
            way = way_of(side)
            post(
                own_b.at[sub, z_at(-way * distance)],
                relay_d.at[sub, k],
                send_d.at[sub, k],
                recv_relay.at[sub, k],
                z_peer(-way * (distance - RELAY)),
            )
        for k, (side, distance) in sorted(enumerate(straight), key=lambda item: -item[1][1]):
            if not has_relay(side, distance):
                send_straight(sub, k, side, distance)

    def has_relay(side, distance):
        return distance == RELAY and any(other == side for other, _ in by_relay)

    def send_straight(sub, k, side, distance):
        way = way_of(side)
        post(
            own_b.at[sub, z_at(-way * distance)],
            in_d.at[sub, k],
            send_d.at[sub, len(by_relay) + k],
            recv_d.at[sub, k],
            z_peer(-way * distance),
        )

    def relay_b(sub):
        for k, (side, distance) in enumerate(straight):
            if has_relay(side, distance):
                spot = z_at(-way_of(side) * distance)
                value = own_b[sub, spot]
                for j, (other, _) in enumerate(by_relay):
                    if other == side:
                        arrived(relay_d.at[sub, j], send_d.at[sub, j], recv_relay.at[sub, j])
                        value += relay_d[sub, j]
                own_b[sub, spot] = value
                send_straight(sub, k, side, distance)

    def gather_b(sub):
        value = own_b[sub, z]
        for k, (side, distance) in enumerate(straight):
            arrived(in_d.at[sub, k], send_d.at[sub, len(by_relay) + k], recv_d.at[sub, k])
            value += in_d[sub, k]
        keep(1, sub, value)

    quarters = []

    def exchange(sub):
        for quarter_id in range(sub * per, (sub + 1) * per):
            for dx in reversed(range(nx)):
                xx = lax.rem(x + dx, nx)
                copy = pltpu.make_async_remote_copy(
                    src_ref=piece.at[xx, quarter_id],
                    dst_ref=got.at[dx, cut],
                    send_sem=send_e.at[dx, quarter_id],
                    recv_sem=recv_e.at[dx, cut],
                    device_id=at(z, y, xx, quarter_id),
                    device_id_type=MESH,
                )
                if dx:
                    copy.start()
                    sends.append(copy)
                else:
                    pl.when(cut != quarter_id)(copy.start)
                    quarters.append((quarter_id, copy))

    events = []
    for sub in range(SUBS):
        events += ring(hops_y, (b0, b1), own_b, send_b, recv_b, sub, local_b, spread_b, y_at, y_peer, 0.01, HOP_Y)
        end = events[-1][0]
        events.append((end + ROUND, functools.partial(relay_b, sub)))
        events.append((end + 2 * ROUND, functools.partial(gather_b, sub)))
        events += ring(hops_z, (a0, a1), own_a, send_a, recv_a, sub, local_a, spread_a, z_at, z_peer, 0.0, HOP_Z)
        events[-1] = (end + 0.1, events[-1][1])
        events.append((end + 1.5 * ROUND, functools.partial(gather_a, sub)))
        events.append((end + 2 * ROUND + 0.1, functools.partial(exchange, sub)))

    pl.semaphore_wait(barrier, len(peers))
    for _, event in sorted(events, key=lambda pair: pair[0]):
        event()

    for dx in range(1, nx):
        xx = lax.rem(x + dx, nx)
        post(piece.at[xx], whole.at[dx], send_whole.at[dx], recv_whole.at[dx], at(z, y, xx, cut))

    entries = dia_ref.shape[1]
    lanes = sum_y.shape[2]
    tile_id = dia_ref[0:1, :]
    code = (
        (dia_ref[3:4, :] * 2 + (tile_id >> 1)) * (nc * nc)
        + dia_ref[1:2, :] * nc
        + dia_ref[2:3, :]
        + (tile_id & 1) * lanes
    ).astype(jnp.float32)
    eye = lax.broadcasted_iota(jnp.int32, (entries, entries), 0) == lax.broadcasted_iota(
        jnp.int32, (entries, entries), 1
    )
    code = jnp.sum(jnp.where(eye, code, 0.0), axis=1, keepdims=True)
    lane_code = lax.broadcasted_iota(jnp.int32, (entries, lanes), 1).astype(jnp.float32)
    pick = [lane_code + float(b * lanes) == code for b in range(2)]

    got[0, cut] = piece[x, cut]
    for t in range(nc):
        for dx in reversed(range(nx)):
            take = functools.partial(arrived, got.at[dx, t], send_e.at[dx, t], recv_e.at[dx, t])
            if dx:
                take()
            else:
                pl.when(cut != t)(take)
    for t in range(nc):
        value = got[0, t]
        for dx in range(1, nx):
            value += got[dx, t]
        total[t] = value

    re = [total[t, 0] for t in range(nc)]
    im = [total[t, 1] for t in range(nc)]

    def down(value):
        return jnp.sum(value, axis=0, keepdims=True)

    rr, ii = {}, {}
    for s in range(nc):
        for t in range(s, nc):
            rr[s, t] = rr[t, s] = down(re[s] * re[t] + im[s] * im[t])
            if s == t:
                ii[s, t] = jnp.zeros_like(rr[s, t])
            else:
                ii[s, t] = down(im[s] * re[t] - re[s] * im[t])
                ii[t, s] = -ii[s, t]
    pairs = [(s, t) for s in range(nc) for t in range(nc)]
    key = z // (nz // (2 * PHASES))
    own_b_col = cut // 2
    lane_id = lax.broadcasted_iota(jnp.int32, (nc * nc, lanes), 1)
    row_id = lax.broadcasted_iota(jnp.int32, (nc * nc, lanes), 0)
    spot = lane_id == key * (nc * nc) + row_id
    tile_rows = lax.broadcasted_iota(jnp.int32, sum_y.shape[1:], 0)
    table = jnp.zeros(sum_y.shape[1:], jnp.float32)
    for part, values in enumerate((rr, ii)):
        column = jnp.sum(jnp.concatenate([values[p] for p in pairs], axis=0), axis=1, keepdims=True)
        lane_row = down(jnp.where(spot, column, 0.0))
        table = jnp.where(tile_rows == 2 * part + own_b_col, lane_row, table)

    def all_sum(table, slots, send_sems, recv_sems, me, count, targets, meanwhile):
        earlier = list(sends)
        sends.clear()
        slots[me] = table
        for k, peer in enumerate(targets):
            post(slots.at[me], slots.at[me], send_sems.at[k], recv_sems.at[me], peer)
        for copy in earlier:
            copy.wait_send()
        meanwhile()
        for k in range(1, count):
            source = lax.rem(me + k, count)
            arrived(slots.at[source], send_sems.at[k - 1], recv_sems.at[source])
        value = slots[0]
        for k in range(1, count):
            value += slots[k]
        return value

    def put_rows():
        rows_own = piece[x]
        for dx in range(1, nx):
            arrived(whole.at[dx], send_whole.at[dx], recv_whole.at[dx])
            rows_own += whole[dx]
        for part in range(2):
            for k in range(nc):
                start = part * modes + k * quarter
                meson_ref[0, :, start : start + quarter] = rows_own[k, part]

    table = all_sum(table, sum_y, send_y, recv_y, y, ny, [at(z, y_at(k), x, cut) for k in far_first(ny)], lambda: None)
    table = all_sum(
        table, sum_x, send_x, recv_x, x * nc + cut, nx * nc, [at(z, y, xx, cc) for xx, cc, _, _ in others], lambda: None
    )
    table = all_sum(table, sum_z, send_z, recv_z, z, nz, [at(z_at(k), y, x, cut) for k in far_first(nz)], put_rows)

    for part in range(2):
        value = jnp.where(pick[0], table[2 * part : 2 * part + 1], 0.0) + jnp.where(
            pick[1], table[2 * part + 1 : 2 * part + 2], 0.0
        )
        column = jnp.sum(value, axis=1, keepdims=True)
        value_ref[part : part + 1, :] = down(jnp.where(eye, column, 0.0)) / TILE

    for copy in sends:
        copy.wait_send()
    for quarter_id, copy in quarters:
        pl.when(cut != quarter_id)(copy.wait_send)


def per_device(vectors, momenta, diagrams):
    nz, ny, nx = RINGS
    modes, sites = vectors.shape[2:]
    rows = PHASES * modes
    rows_y = rows // (nz * ny)
    rows_z = rows_y * ny
    width = modes // SUBS
    quarter = modes // CUTS
    lanes = max(128, 2 * PHASES * CUTS * CUTS)
    depth = 6 * sites
    z_hops, y_hops = meet(nz), meet(ny)
    by_relay, straight = relays(nz)
    f32, bf16 = jnp.float32, jnp.bfloat16
    dma = pltpu.SemaphoreType.DMA

    def slots(hops, *shape):
        return [pltpu.VMEM((count + 1, SUBS, *shape), f32) for count in hops]

    def sems(hops):
        return [dma((2, hops[0], SUBS))] * 2

    scratch = [
        pltpu.VMEM(vectors.shape[1:], f32),
        pltpu.VMEM((nz, ny, rows_y, depth), bf16),
        pltpu.VMEM((2 * modes, depth), bf16),
        *slots(z_hops, rows_z, width),
        *slots(y_hops, nz * rows_y, width),
        pltpu.VMEM((SUBS, ny, rows_y, width), f32),
        pltpu.VMEM((SUBS, nz, rows_y, width), f32),
        pltpu.VMEM((SUBS, ny - 1, rows_y, width), f32),
        pltpu.VMEM((SUBS, max(1, len(by_relay)), rows_y, width), f32),
        pltpu.VMEM((SUBS, len(straight), rows_y, width), f32),
        pltpu.VMEM((nx, CUTS, 2, rows_y // nx, quarter), f32),
        pltpu.VMEM((nx, CUTS, 2, rows_y // nx, quarter), f32),
        pltpu.VMEM((nx, CUTS, 2, rows_y // nx, quarter), f32),
        pltpu.VMEM((CUTS, 2, rows_y // nx, quarter), f32),
        pltpu.VMEM((ny, 8, lanes), f32),
        pltpu.VMEM((nx * CUTS, 8, lanes), f32),
        pltpu.VMEM((nz, 8, lanes), f32),
        dma,
        *sems(z_hops),
        *sems(y_hops),
        *[dma((SUBS, ny - 1))] * 2,
        dma((SUBS, nz - 1)),
        dma((SUBS, max(1, len(by_relay)))),
        dma((SUBS, len(straight))),
        *[dma((nx, CUTS))] * 2,
        *[dma((nx,))] * 2,
        *[dma((ny,))] * 2,
        *[dma((nx * CUTS,))] * 2,
        *[dma((nz,))] * 2,
    ]
    vmem = pl.BlockSpec(memory_space=pltpu.VMEM)
    meson, values = pl.pallas_call(
        kernel,
        out_shape=(
            pltpu.VMEM((1, rows_y // nx, 2 * modes), f32),
            pltpu.VMEM((2, diagrams.shape[0]), f32),
        ),
        in_specs=[pl.BlockSpec(memory_space=pl.ANY), pl.BlockSpec(memory_space=pltpu.SMEM), vmem],
        out_specs=(vmem, vmem),
        scratch_shapes=scratch,
        compiler_params=pltpu.CompilerParams(
            collective_id=0, has_side_effects=True, vmem_limit_bytes=56 * 1024 * 1024
        ),
    )(vectors, momenta, diagrams.T)
    return meson, values.T


def solution(mesh):
    return jax.shard_map(
        per_device,
        mesh=mesh,
        in_specs=(P("cuts", None, None, "space"), P(), P()),
        out_specs=(P("cuts", "space", None), P()),
        check_vma=False,
    )
```
